256 devices in a mesh: batch: 32 (over z_lo, x, y), strip: 8 (over z_hi, core).
Axes of the slice: x: 4, y: 4, z: 8 (z_hi: 4, z_lo: 2; z = z_hi * 2 + z_lo), core: 2. Of those that a mesh axis runs over, the one named last changes fastest.
Arguments:
- state_maps: bfloat16 [32, 128, 64, 256], P('batch', 'strip'), may hold values from -6 to 6
- goal_maps: bfloat16 [32, 128, 64, 256], P('batch', 'strip'), may hold values from -6 to 6
- conv_one: bfloat16 [3, 3, 256, 256], replicated, may hold values from -0.125 to 0.125
- conv_two: bfloat16 [3, 3, 256, 256], replicated, may hold values from -0.125 to 0.125
- state_proj: bfloat16 [256, 1024], replicated, may hold values from -0.375 to 0.375
- goal_proj: bfloat16 [256, 1024], replicated, may hold values from -0.375 to 0.375
- inv_temp: float32 [1], replicated, may hold values from 4 to 16
- pair_index: int32 [32], P('batch'), may hold values from 0 to 31, each once
Outputs:
- pair_loss: float32 [32], P('batch')
- grad_state_proj: float32 [256, 1024], replicated
- grad_goal_proj: float32 [256, 1024], replicated
- block_maps: float32 [2, 32, 128, 64, 256], P(None, 'batch', 'strip')
The draws below stay inside these ranges and needn't reach their ends.
Inputs may be any that keep to these rules, and one draw needn't show every extreme that they name: pair_index names each goal of 0 to 31 exactly once.
All inputs are finite; a program needn't handle non-finite values.
Results may differ from the reference program's by a relative error of at most 0.017.
Values may be sent and summed in bfloat16 or wider, within the bound.
No kernel may reach another device: no remote copies, remote signals or barrier semaphores. Data moves between devices by JAX's collectives and lax.ppermute only.
A program may use at most 64 MiB of HBM per device.

```python
import jax
import jax.numpy as jnp
from jax import lax

C = 256
E = 1024
COLS = 64
ROWS = 128
PAIRS = 32


def maps_draw(base_key):
    first_key, second_key = jax.random.split(base_key, 2)
    full_shape = (PAIRS, ROWS, COLS, C)
    rough_part = jax.random.normal(first_key, full_shape, jnp.float32)
    offset = jax.random.normal(second_key, (PAIRS, 1, 1, C), jnp.float32)
    return jnp.clip(0.7 * rough_part + offset, -6.0, 6.0).astype(jnp.bfloat16)


def draw_state_maps(key, part):
    return maps_draw(jax.random.fold_in(key, 11))


def draw_goal_maps(key, part):
    return maps_draw(jax.random.fold_in(key, 23))


def centred(own_key, extent, deviation, bound, kind=jnp.bfloat16):
    return jnp.clip(deviation * jax.random.normal(own_key, extent, jnp.float32), -bound, bound).astype(kind)


def setup_inputs(seed: int = 0) -> dict:
    keys = jax.random.split(jax.random.key(seed), 9)
    return {
        "state_maps": draw_state_maps(jax.random.fold_in(keys[8], 71), 0),
        "goal_maps": draw_goal_maps(jax.random.fold_in(keys[8], 71), 0),
        "conv_one": centred(keys[2], (3, 3, C, C), (9 * C) ** -0.5, 0.125),
        "conv_two": centred(keys[3], (3, 3, C, C), (9 * C) ** -0.5, 0.125),
        "state_proj": centred(keys[4], (C, E), C ** -0.5, 0.375),
        "goal_proj": centred(keys[5], (C, E), C ** -0.5, 0.375),
        "inv_temp": jnp.clip(jax.random.uniform(keys[6], (1,), jnp.float32, 4.0, 16.0), 4.0, 16.0),
        "pair_index": jax.random.permutation(keys[7], PAIRS).astype(jnp.int32),
    }


def conv_same(frame_maps, kernel):
    return lax.conv_general_dilated(frame_maps.astype(jnp.float32), kernel.astype(jnp.float32), (1, 1), ((1, 1), (1, 1)), dimension_numbers=('NHWC', 'HWIO', 'NHWC'), precision=lax.Precision.HIGHEST)

def encode(frame_maps, conv_one, conv_two):
    active = jnp.maximum(frame_maps, 0)
    first_out = jnp.maximum(conv_same(active, conv_one), 0.0).astype(jnp.bfloat16)
    block_out = jnp.maximum(frame_maps.astype(jnp.float32) + conv_same(first_out, conv_two), 0.0)
    return (lax.optimization_barrier(jnp.mean(block_out, axis=(1, 2))), block_out)

def pooled_all(frame_maps, conv_one, conv_two):
    grouped = frame_maps.reshape((PAIRS, 1) + frame_maps.shape[1:])
    pooled, block_out = lax.map(lambda block: encode(block, conv_one, conv_two), grouped)
    return (pooled.reshape(PAIRS, C), block_out.reshape(frame_maps.shape))

def normalize(embedding):
    inverse_norm = lax.rsqrt(lax.optimization_barrier(jnp.sum(embedding * embedding, axis=-1, keepdims=True)) + 1e-06)
    return (embedding * inverse_norm, inverse_norm)

def reference(state_maps, goal_maps, conv_one, conv_two, state_proj, goal_proj, inv_temp, pair_index):
    state_pooled, state_block = pooled_all(state_maps, conv_one, conv_two)
    goal_pooled, goal_block = pooled_all(goal_maps, conv_one, conv_two)
    block_maps = jnp.stack([state_block, goal_block], axis=0)
    state_pool = state_pooled.astype(jnp.bfloat16)
    goal_pool = goal_pooled.astype(jnp.bfloat16)
    state_emb = jnp.dot(state_pool, state_proj, preferred_element_type=jnp.float32)
    goal_emb = jnp.dot(goal_pool, goal_proj, preferred_element_type=jnp.float32)
    state_unit, state_inverse = normalize(state_emb)
    goal_unit, goal_inverse = normalize(goal_emb)
    state_bf = state_unit.astype(jnp.bfloat16)
    goal_bf = goal_unit.astype(jnp.bfloat16)
    sharpness = inv_temp[0]
    logits = sharpness * jnp.dot(state_bf, goal_bf.T, preferred_element_type=jnp.float32)
    exp_logits = jnp.exp(logits)
    row_total = lax.optimization_barrier(jnp.sum(exp_logits, axis=1))
    matched = jnp.arange(PAIRS, dtype=jnp.int32)[None, :] == pair_index[:, None]
    positive = lax.optimization_barrier(jnp.sum(jnp.where(matched, logits, 0.0), axis=1))
    pair_loss = jnp.log(row_total) - positive
    logit_grad = (exp_logits / row_total[:, None] - matched.astype(jnp.float32)).astype(jnp.bfloat16)
    state_unit_grad = sharpness * jnp.dot(logit_grad, goal_bf, preferred_element_type=jnp.float32)
    goal_unit_grad = sharpness * jnp.dot(logit_grad.T, state_bf, preferred_element_type=jnp.float32)
    state_emb_grad = ((state_unit_grad - state_unit * lax.optimization_barrier(jnp.sum(state_unit * state_unit_grad, axis=-1, keepdims=True))) * state_inverse).astype(jnp.bfloat16)
    goal_emb_grad = ((goal_unit_grad - goal_unit * lax.optimization_barrier(jnp.sum(goal_unit * goal_unit_grad, axis=-1, keepdims=True))) * goal_inverse).astype(jnp.bfloat16)
    grad_state_proj = jnp.dot(state_pool.T, state_emb_grad, preferred_element_type=jnp.float32)
    grad_goal_proj = jnp.dot(goal_pool.T, goal_emb_grad, preferred_element_type=jnp.float32)
    return (pair_loss, grad_state_proj, grad_goal_proj, block_maps)
```

```python
import functools
import jax
import jax.numpy as jnp
from jax import lax
from jax.experimental import pallas as pl
from jax.experimental.pallas import tpu as pltpu
from jax.sharding import PartitionSpec as P

ROWS, COLS, C, E = 16, 64, 256, 1024
BF, F32 = jnp.bfloat16, jnp.float32
MIB = 1 << 20


def widen(row):
    col = lax.broadcasted_iota(jnp.int32, row.shape, 0)
    left = jnp.where(col == 0, 0.0, pltpu.roll(row, 1, 0))
    right = jnp.where(col == COLS - 1, 0.0, pltpu.roll(row, COLS - 1, 0))
    return jnp.concatenate([left.astype(BF), row.astype(BF), right.astype(BF)], axis=-1)


def conv(wide, first, rows, weights):
    total = None
    for dy in range(3):
        lhs = wide[pl.ds(first + dy, rows)].reshape(rows * COLS, 3 * C)
        part = jnp.dot(lhs, weights[dy], preferred_element_type=F32)
        total = part if total is None else total + part
    return total


def interior_kernel(step1, step2, s_hbm, g_hbm, w1_hbm, w2_hbm, out_hbm, edge_ref, sum_ref,
                    x, w1, w2, xw, hw, o, sems, osem):
    cx = [pltpu.make_async_copy(ref.at[0], x.at[f], sems.at[f]) for f, ref in enumerate((s_hbm, g_hbm))]
    cw1 = pltpu.make_async_copy(w1_hbm, w1, sems.at[2])
    cw2 = pltpu.make_async_copy(w2_hbm, w2, sems.at[3])
    cx[0].start(); cw1.start(); cx[1].start(); cw2.start()
    outs = []
    for f in range(2):
        cx[f].wait()
        for r in range(ROWS):
            xw[f, r] = widen(jnp.maximum(x[f, r].astype(F32), 0.0))
        if f == 0:
            cw1.wait()
        for r in range(0, 14, step1):
            h = jnp.maximum(conv(xw.at[f], r, step1, w1), 0.0)
            for k in range(step1):
                hw[f, r + k] = widen(h[k * COLS:(k + 1) * COLS])
        if f == 0:
            cw2.wait()
        acc = None
        for r in range(0, 12, step2):
            y = conv(hw.at[f], r, step2, w2)
            y = jnp.maximum(y + x[f, r + 2:r + 2 + step2].reshape(step2 * COLS, C).astype(F32), 0.0)
            o[f, r:r + step2] = y.reshape(step2, COLS, C)
            part = jnp.sum(y.reshape(step2 * COLS // 8, 8, C), axis=0)
            acc = part if acc is None else acc + part
        sum_ref[f] = acc
        for k, r in enumerate((0, 1, 12, 13)):
            edge_ref[2 * f + k // 2, k % 2] = hw[f, r, :, C:2 * C]
        cp = pltpu.make_async_copy(o.at[f], out_hbm.at[f, 0, pl.ds(2, 12)], osem.at[f])
        cp.start()
        outs.append(cp)
    for cp in outs:
        cp.wait()


def interior(s, g, w1, w2, step1=7, step2=6):
    anyspec = pl.BlockSpec(memory_space=pl.ANY)
    vm = pl.BlockSpec(memory_space=pltpu.VMEM)
    return pl.pallas_call(
        functools.partial(interior_kernel, step1, step2),
        name="interior_rows",
        out_shape=(jax.ShapeDtypeStruct((2, 1, ROWS, COLS, C), F32),
                   jax.ShapeDtypeStruct((4, 2, COLS, C), BF),
                   jax.ShapeDtypeStruct((2, 8, C), F32)),
        in_specs=[anyspec] * 4,
        out_specs=(anyspec, vm, vm),
        scratch_shapes=[
            pltpu.VMEM((2, ROWS, COLS, C), BF),
            pltpu.VMEM((3, 3 * C, C), BF),
            pltpu.VMEM((3, 3 * C, C), BF),
            pltpu.VMEM((2, ROWS, COLS, 3 * C), BF),
            pltpu.VMEM((2, 14, COLS, 3 * C), BF),
            pltpu.VMEM((2, 12, COLS, C), F32),
            pltpu.SemaphoreType.DMA((4,)),
            pltpu.SemaphoreType.DMA((2,)),
        ],
        compiler_params=pltpu.CompilerParams(vmem_limit_bytes=40 * MIB),
        cost_estimate=pl.CostEstimate(flops=4_200_000_000, transcendentals=0, bytes_accessed=6_000_000),
    )(s, g, w1, w2)


def edge_kernel(here, s_hbm, g_hbm, above_hbm, below_hbm, hedge, sums, w1_hbm, w2_hbm, out_in, out_hbm, sum_ref,
                xe, w1, w2, xw, hw, o, sems, osem):
    copies = []
    for f, ref in enumerate((s_hbm, g_hbm)):
        copies.append(pltpu.make_async_copy(above_hbm.at[f], xe.at[2 * f, pl.ds(0, 2)], sems.at[len(copies)]))
        copies.append(pltpu.make_async_copy(ref.at[0, pl.ds(0, 2)], xe.at[2 * f, pl.ds(2, 2)], sems.at[len(copies)]))
        copies.append(pltpu.make_async_copy(ref.at[0, pl.ds(14, 2)], xe.at[2 * f + 1, pl.ds(0, 2)], sems.at[len(copies)]))
        copies.append(pltpu.make_async_copy(below_hbm.at[f], xe.at[2 * f + 1, pl.ds(2, 2)], sems.at[len(copies)]))
    cw1 = pltpu.make_async_copy(w1_hbm, w1, sems.at[8])
    cw2 = pltpu.make_async_copy(w2_hbm, w2, sems.at[9])
    for cp in copies:
        cp.start()
    cw1.start(); cw2.start()
    for cp in copies:
        cp.wait()
    for k in range(4):
        for r in range(4):
            xw[r, k] = widen(jnp.maximum(xe[k, r].astype(F32), 0.0))
    for k in range(4):
        for r in range(2):
            hw[r + 2 * (1 - k % 2), k] = widen(hedge[k, r].astype(F32))
    cw1.wait()

    def conv4(wide, weights):
        total = None
        for dy in range(3):
            lhs = wide[pl.ds(dy, 2)].reshape(2 * 4 * COLS, 3 * C)
            part = jnp.dot(lhs, weights[dy], preferred_element_type=F32)
            total = part if total is None else total + part
        return total

    h = jnp.maximum(conv4(xw, w1), 0.0)
    for r in range(2):
        for k in range(4):
            row = h[(r * 4 + k) * COLS:(r * 4 + k + 1) * COLS]
            if k % 2 == 0 and r == 0:
                row = jnp.where(here[0] > 0, row, 0.0)
            if k % 2 == 1 and r == 1:
                row = jnp.where(here[0] < here[1] - 1, row, 0.0)
            hw[r + 2 * (k % 2), k] = widen(row)
    cw2.wait()
    y = conv4(hw, w2)
    tot = [sums[0], sums[1]]
    outs = []
    for k in range(4):
        f = k // 2
        for r in range(2):
            v = y[(r * 4 + k) * COLS:(r * 4 + k + 1) * COLS] + xe[k, r + 2 * (1 - k % 2)].astype(F32)
            v = jnp.maximum(v, 0.0)
            o[k, r] = v
            tot[f] = tot[f] + jnp.sum(v.reshape(8, 8, C), axis=0)
        cp = pltpu.make_async_copy(o.at[k], out_hbm.at[f, 0, pl.ds(14 * (k % 2), 2)], osem.at[k])
        cp.start()
        outs.append(cp)
    for f in range(2):
        sum_ref[f:f + 1] = jnp.sum(tot[f], axis=0, keepdims=True)
    for cp in outs:
        cp.wait()


def edges(here, s, g, above, below, hedge, sums, w1, w2, out):
    anyspec = pl.BlockSpec(memory_space=pl.ANY)
    vm = pl.BlockSpec(memory_space=pltpu.VMEM)
    return pl.pallas_call(
        edge_kernel,
        name="edge_rows",
        out_shape=(jax.ShapeDtypeStruct(out.shape, F32), jax.ShapeDtypeStruct((2, C), F32)),
        in_specs=[pl.BlockSpec(memory_space=pltpu.SMEM)] + [anyspec] * 4 + [vm] * 2 + [anyspec] * 3,
        out_specs=(anyspec, vm),
        input_output_aliases={9: 0},
        scratch_shapes=[
            pltpu.VMEM((4, 4, COLS, C), BF),
            pltpu.VMEM((3, 3 * C, C), BF),
            pltpu.VMEM((3, 3 * C, C), BF),
            pltpu.VMEM((4, 4, COLS, 3 * C), BF),
            pltpu.VMEM((4, 4, COLS, 3 * C), BF),
            pltpu.VMEM((4, 2, COLS, C), F32),
            pltpu.SemaphoreType.DMA((10,)),
            pltpu.SemaphoreType.DMA((4,)),
        ],
        compiler_params=pltpu.CompilerParams(vmem_limit_bytes=24 * MIB),
        cost_estimate=pl.CostEstimate(flops=1_200_000_000, transcendentals=0, bytes_accessed=4_000_000),
    )(here, s, g, above, below, hedge, sums, w1, w2, out)
def head_kernel(mine, sharp, tot, sproj, gproj, loss_ref, gs_hbm, gg_hbm, buf, sem):
    pairs = tot.shape[1]
    s_pool = tot[0, :, :C].astype(BF)
    g_pool = tot[1, :, :C].astype(BF)
    label = tot[0, :, C:C + 1]
    temp = sharp[0]
    s_emb = jnp.dot(s_pool, sproj[...], preferred_element_type=F32)
    g_emb = jnp.dot(g_pool, gproj[...], preferred_element_type=F32)
    s_inv = lax.rsqrt(jnp.sum(s_emb * s_emb, axis=-1, keepdims=True) + 1e-06)
    g_inv = lax.rsqrt(jnp.sum(g_emb * g_emb, axis=-1, keepdims=True) + 1e-06)
    s_unit = s_emb * s_inv
    g_unit = g_emb * g_inv
    s_bf = s_unit.astype(BF)
    g_bf = g_unit.astype(BF)
    logits = temp * lax.dot_general(s_bf, g_bf, (((1,), (1,)), ((), ())), preferred_element_type=F32)
    ex = jnp.exp(logits)
    row_total = jnp.sum(ex, axis=1, keepdims=True)
    column = lax.broadcasted_iota(jnp.int32, (pairs, pairs), 1).astype(F32)
    matched = column == label
    positive = jnp.sum(jnp.where(matched, logits, 0.0), axis=1, keepdims=True)
    losses = jnp.log(row_total) - positive
    row = lax.broadcasted_iota(jnp.int32, (pairs, 1), 0)
    loss_ref[0] = jnp.sum(jnp.where(row == mine[0], losses, 0.0))
    lgrad = (ex / row_total - jnp.where(matched, 1.0, 0.0)).astype(BF)
    s_ug = temp * jnp.dot(lgrad, g_bf, preferred_element_type=F32)
    g_ug = temp * lax.dot_general(lgrad, s_bf, (((0,), (0,)), ((), ())), preferred_element_type=F32)
    s_eg = ((s_ug - s_unit * jnp.sum(s_unit * s_ug, axis=-1, keepdims=True)) * s_inv).astype(BF)
    g_eg = ((g_ug - g_unit * jnp.sum(g_unit * g_ug, axis=-1, keepdims=True)) * g_inv).astype(BF)
    outs = []
    for k, (pool, grad, dest) in enumerate(((s_pool, s_eg, gs_hbm), (g_pool, g_eg, gg_hbm))):
        buf[k] = lax.dot_general(pool, grad, (((0,), (0,)), ((), ())), preferred_element_type=F32)
        cp = pltpu.make_async_copy(buf.at[k], dest, sem.at[k])
        cp.start()
        outs.append(cp)
    for cp in outs:
        cp.wait()


def head(mine, sharp, tot, sproj, gproj):
    anyspec = pl.BlockSpec(memory_space=pl.ANY)
    vm = pl.BlockSpec(memory_space=pltpu.VMEM)
    sm = pl.BlockSpec(memory_space=pltpu.SMEM)
    return pl.pallas_call(
        head_kernel,
        name="contrastive_head",
        out_shape=(jax.ShapeDtypeStruct((1,), F32), jax.ShapeDtypeStruct((C, E), F32),
                   jax.ShapeDtypeStruct((C, E), F32)),
        in_specs=[sm, sm, vm, vm, vm],
        out_specs=(sm, anyspec, anyspec),
        scratch_shapes=[pltpu.VMEM((2, C, E), F32), pltpu.SemaphoreType.DMA((2,))],
        compiler_params=pltpu.CompilerParams(vmem_limit_bytes=16 * MIB),
    )(mine, sharp, tot, sproj, gproj)


def shards(state_maps, goal_maps, conv_one, conv_two, state_proj, goal_proj, inv_temp, pair_index):
    strips, batch = lax.axis_size("strip"), lax.axis_size("batch")
    here = lax.axis_index("strip").astype(jnp.int32)
    mine = lax.axis_index("batch").astype(jnp.int32)
    w1 = conv_one.reshape(3, 3 * C, C)
    w2 = conv_two.reshape(3, 3 * C, C)
    down = [(i, i + 1) for i in range(strips - 1)]
    up = [(i + 1, i) for i in range(strips - 1)]
    tails = jnp.concatenate([state_maps[:, ROWS - 2:], goal_maps[:, ROWS - 2:]], axis=0)
    heads = jnp.concatenate([state_maps[:, :2], goal_maps[:, :2]], axis=0)
    above = lax.ppermute(tails, "strip", down)
    below = lax.ppermute(heads, "strip", up)
    out, hedge, sums = interior(state_maps, goal_maps, w1, w2)
    place = jnp.stack([here, jnp.full((), strips, jnp.int32)])
    out, total = edges(place, state_maps, goal_maps, above, below, hedge, sums, w1, w2, out)
    label = jnp.full((2, 128), pair_index[0].astype(F32))
    share = jnp.concatenate([total * (1.0 / (strips * ROWS * COLS)), label], axis=1)
    pair_groups = [[2 * i, 2 * i + 1] for i in range(strips // 2)]
    share = lax.psum(share, "strip", axis_index_groups=pair_groups).astype(BF)
    groups = [[b * strips + s for b in range(batch) for s in range(core, strips, 2)] for core in range(2)]
    members = batch * strips // 2
    copies = jnp.broadcast_to(share, (members, *share.shape))
    got = lax.all_to_all(copies, ("batch", "strip"), 0, 0, tiled=True, axis_index_groups=groups)
    got = got.reshape(batch, strips // 2, 2, C + 128).astype(F32)
    tot = jnp.moveaxis(jnp.sum(got, axis=1), 1, 0)
    tot = tot * jnp.where(jnp.arange(C + 128) < C, 1.0, 1.0 / strips)
    loss, gs, gg = head(mine.reshape(1), inv_temp, tot, state_proj, goal_proj)
    return (loss, gs, gg, out)


def solution(mesh):
    placed = (
        P("batch", "strip", None, None),
        P("batch", "strip", None, None),
        P(),
        P(),
        P(),
        P(),
        P(),
        P("batch"),
    )
    return jax.shard_map(
        shards,
        mesh=mesh,
        in_specs=placed,
        out_specs=(P("batch"), P(), P(), P(None, "batch", "strip", None, None)),
        check_vma=False,
    )
```

```python
import functools
import jax
import jax.numpy as jnp
from jax import lax
from jax.experimental import pallas as pl
from jax.experimental.pallas import tpu as pltpu
from jax.sharding import PartitionSpec as P

ROWS, COLS, C, E = 16, 64, 256, 1024
BF, F32 = jnp.bfloat16, jnp.float32
MIB = 1 << 20
HBM = pl.BlockSpec(memory_space=pltpu.MemorySpace.HBM)
VM = pl.BlockSpec(memory_space=pltpu.MemorySpace.VMEM)
SM = pl.BlockSpec(memory_space=pltpu.MemorySpace.SMEM)


def pack_kernel(here, s_hbm, g_hbm, chip, cross, sems):
    odd = lax.rem(here[0], 2)
    copies = []
    for f, ref in enumerate((s_hbm, g_hbm)):
        tail = (ROWS - 2) * (1 - odd)
        head = (ROWS - 2) * odd
        copies.append(pltpu.make_async_copy(ref.at[0, pl.ds(tail, 2)], chip.at[f], sems.at[f]))
        copies.append(pltpu.make_async_copy(ref.at[0, pl.ds(head, 2)], cross.at[f], sems.at[2 + f]))
    for cp in copies:
        cp.start()
    for cp in copies:
        cp.wait()


def pack(here, s, g):
    side = jax.ShapeDtypeStruct((2, 2, COLS, C), BF)
    return pl.pallas_call(
        pack_kernel,
        name="pack_halo_rows",
        out_shape=(side, side),
        in_specs=[SM, HBM, HBM],
        out_specs=(VM, VM),
        scratch_shapes=[pltpu.SemaphoreType.DMA((4,))],
        compiler_params=pltpu.CompilerParams(vmem_limit_bytes=2 * MIB),
    )(here, s, g)


def widen(row):
    col = lax.broadcasted_iota(jnp.int32, row.shape, 0)
    left = jnp.where(col == 0, 0.0, pltpu.roll(row, 1, 0))
    right = jnp.where(col == COLS - 1, 0.0, pltpu.roll(row, COLS - 1, 0))
    return jnp.concatenate([left.astype(BF), row.astype(BF), right.astype(BF)], axis=-1)


def conv(wide, first, rows, weights):
    total = None
    for dy in range(3):
        lhs = wide[pl.ds(first + dy, rows)].reshape(rows * COLS, 3 * C)
        part = jnp.dot(lhs, weights[dy], preferred_element_type=F32)
        total = part if total is None else total + part
    return total


def conv_of(rows, weights):
    total = None
    for dy in range(3):
        lhs = jnp.concatenate([rows[dy], rows[dy + 1]], axis=0)
        part = jnp.dot(lhs, weights[dy], preferred_element_type=F32)
        total = part if total is None else total + part
    return total


def spans(total, step):
    return [(r, min(step, total - r)) for r in range(0, total, step)]


def interior_kernel(step1, step2, s_hbm, g_hbm, w1_hbm, w2_hbm, x, xw, hw, o, sum_ref, w1, w2, sems):
    cx = [[pltpu.make_async_copy(ref.at[0, pl.ds(8 * p, 8)], x.at[f, pl.ds(8 * p, 8)], sems.at[2 * f + p])
           for p in range(2)] for f, ref in enumerate((s_hbm, g_hbm))]
    cw1 = pltpu.make_async_copy(w1_hbm, w1, sems.at[4])
    cw2 = pltpu.make_async_copy(w2_hbm, w2, sems.at[5])
    cx[0][0].start(); cw1.start(); cx[0][1].start(); cw2.start(); cx[1][0].start(); cx[1][1].start()

    def spread(f, rows):
        for r in rows:
            xw[f, r] = widen(jnp.maximum(x[f, r].astype(F32), 0.0))

    def first(f, r, n):
        h = jnp.maximum(conv(xw.at[f], r, n, w1), 0.0)
        for k in range(n):
            hw[f, r + k] = widen(h[k * COLS:(k + 1) * COLS])

    def second(f, r, n, acc):
        y = conv(hw.at[f], r, n, w2)
        y = jnp.maximum(y + x[f, r + 2:r + 2 + n].reshape(n * COLS, C).astype(F32), 0.0)
        o[f, r:r + n] = y.reshape(n, COLS, C)
        part = jnp.sum(y.reshape(n * COLS // 8, 8, C), axis=0)
        return part if acc is None else acc + part

    cx[0][0].wait()
    spread(0, range(8))
    cx[0][1].wait()
    spread(0, range(8, 16))
    cw1.wait()
    for r, n in spans(14, step1):
        first(0, r, n)
    cx[1][0].wait(); cx[1][1].wait(); cw2.wait()
    acc = None
    todo = list(range(16))
    plan = spans(12, step2)
    for i, (r, n) in enumerate(plan):
        share = todo[i * 16 // len(plan):(i + 1) * 16 // len(plan)]
        spread(1, share)
        acc = second(0, r, n, acc)
    sum_ref[0] = acc
    for r, n in spans(14, step1):
        first(1, r, n)
    acc = None
    for r, n in spans(12, step2):
        acc = second(1, r, n, acc)
    sum_ref[1] = acc


def interior(s, g, w1, w2, step1=7, step2=6):
    wide = jax.ShapeDtypeStruct((3, 3 * C, C), BF)
    return pl.pallas_call(
        functools.partial(interior_kernel, step1, step2),
        name="interior_rows",
        out_shape=(jax.ShapeDtypeStruct((2, ROWS, COLS, C), BF),
                   jax.ShapeDtypeStruct((2, ROWS, COLS, 3 * C), BF),
                   jax.ShapeDtypeStruct((2, 14, COLS, 3 * C), BF),
                   jax.ShapeDtypeStruct((2, 12, COLS, C), F32),
                   jax.ShapeDtypeStruct((2, 8, C), F32), wide, wide),
        in_specs=[HBM] * 4,
        out_specs=(VM,) * 7,
        scratch_shapes=[pltpu.SemaphoreType.DMA((6,))],
        compiler_params=pltpu.CompilerParams(vmem_limit_bytes=24 * MIB),
        cost_estimate=pl.CostEstimate(flops=4_200_000_000, transcendentals=0, bytes_accessed=6_000_000),
    )(s, g, w1, w2)


def edge_kernel(here, chip, cross, x, xw, hw, sums, w1, w2, sp_hbm, gp_hbm, o, share, sp, gp, halo, hh, sems):
    csp = pltpu.make_async_copy(sp_hbm, sp, sems.at[0])
    cgp = pltpu.make_async_copy(gp_hbm, gp, sems.at[1])
    csp.start(); cgp.start()
    odd = lax.rem(here[0], 2)
    for f in range(2):
        for r in range(2):
            a = widen(jnp.maximum(chip[f, r].astype(F32), 0.0))
            b = widen(jnp.maximum(cross[f, r].astype(F32), 0.0))
            halo[2 * f + 1 - odd, r] = a
            halo[2 * f + odd, r] = b
    for k in range(4):
        f = k // 2
        if k % 2 == 0:
            rows = [halo[k, 0], halo[k, 1], xw[f, 0], xw[f, 1]]
        else:
            rows = [xw[f, ROWS - 2], xw[f, ROWS - 1], halo[k, 0], halo[k, 1]]
        h = jnp.maximum(conv_of(rows, w1), 0.0)
        for r in range(2):
            row = h[r * COLS:(r + 1) * COLS]
            if k % 2 == 0 and r == 0:
                row = jnp.where(here[0] > 0, row, 0.0)
            if k % 2 == 1 and r == 1:
                row = jnp.where(here[0] < here[1] - 1, row, 0.0)
            hh[k, r] = widen(row)
    tot = [sums[0], sums[1]]
    for k in range(4):
        f = k // 2
        if k % 2 == 0:
            rows = [hh[k, 0], hh[k, 1], hw[f, 0], hw[f, 1]]
        else:
            rows = [hw[f, 12], hw[f, 13], hh[k, 0], hh[k, 1]]
        y = conv_of(rows, w2)
        y = jnp.maximum(y + x[f, 14 * (k % 2):14 * (k % 2) + 2].reshape(2 * COLS, C).astype(F32), 0.0)
        o[k] = y.reshape(2, COLS, C)
        tot[f] = tot[f] + jnp.sum(y.reshape(16, 8, C), axis=0)
    scale = 1.0 / (here[1] * (ROWS * COLS)).astype(F32)
    for f in range(2):
        share[f:f + 1, :C] = jnp.sum(tot[f], axis=0, keepdims=True) * scale
    share[:, C:] = jnp.full((2, 128), here[2], jnp.int32).astype(F32)
    csp.wait(); cgp.wait()


def edges(here, chip, cross, x, xw, hw, sums, w1, w2, sp, gp):
    proj = jax.ShapeDtypeStruct((C, E), BF)
    return pl.pallas_call(
        edge_kernel,
        name="edge_rows",
        out_shape=(jax.ShapeDtypeStruct((4, 2, COLS, C), F32), jax.ShapeDtypeStruct((2, C + 128), F32), proj, proj),
        in_specs=[SM] + [VM] * 8 + [HBM] * 2,
        out_specs=(VM,) * 4,
        scratch_shapes=[
            pltpu.VMEM((4, 2, COLS, 3 * C), BF),
            pltpu.VMEM((4, 2, COLS, 3 * C), BF),
            pltpu.SemaphoreType.DMA((2,)),
        ],
        compiler_params=pltpu.CompilerParams(vmem_limit_bytes=24 * MIB),
        cost_estimate=pl.CostEstimate(flops=1_200_000_000, transcendentals=0, bytes_accessed=4_000_000),
    )(here, chip, cross, x, xw, hw, sums, w1, w2, sp, gp)


def head_kernel(mine, sharp, tot, sproj, gproj, o, oe, loss_ref, gs_hbm, gg_hbm, out_hbm, buf, sem, osem):
    outs = []
    for f in range(2):
        outs.append(pltpu.make_async_copy(o.at[f], out_hbm.at[f, 0, pl.ds(2, 12)], osem.at[3 * f]))
        for k in range(2):
            outs.append(pltpu.make_async_copy(oe.at[2 * f + k], out_hbm.at[f, 0, pl.ds(14 * k, 2)], osem.at[3 * f + 1 + k]))
    for cp in outs:
        cp.start()
    pairs = tot.shape[1]
    s_pool = tot[0, :, :C].astype(BF)
    g_pool = tot[1, :, :C].astype(BF)
    label = tot[0, :, C:C + 1]
    temp = sharp[0]
    s_emb = jnp.dot(s_pool, sproj[...], preferred_element_type=F32)
    g_emb = jnp.dot(g_pool, gproj[...], preferred_element_type=F32)
    s_inv = lax.rsqrt(jnp.sum(s_emb * s_emb, axis=-1, keepdims=True) + 1e-06)
    g_inv = lax.rsqrt(jnp.sum(g_emb * g_emb, axis=-1, keepdims=True) + 1e-06)
    s_unit = s_emb * s_inv
    g_unit = g_emb * g_inv
    s_bf = s_unit.astype(BF)
    g_bf = g_unit.astype(BF)
    logits = temp * lax.dot_general(s_bf, g_bf, (((1,), (1,)), ((), ())), preferred_element_type=F32)
    ex = jnp.exp(logits)
    row_total = jnp.sum(ex, axis=1, keepdims=True)
    column = lax.broadcasted_iota(jnp.int32, (pairs, pairs), 1).astype(F32)
    matched = column == label
    positive = jnp.sum(jnp.where(matched, logits, 0.0), axis=1, keepdims=True)
    losses = jnp.log(row_total) - positive
    row = lax.broadcasted_iota(jnp.int32, (pairs, 1), 0)
    lgrad = (ex / row_total - jnp.where(matched, 1.0, 0.0)).astype(BF)
    s_ug = temp * jnp.dot(lgrad, g_bf, preferred_element_type=F32)
    g_ug = temp * lax.dot_general(lgrad, s_bf, (((0,), (0,)), ((), ())), preferred_element_type=F32)
    s_eg = ((s_ug - s_unit * jnp.sum(s_unit * s_ug, axis=-1, keepdims=True)) * s_inv).astype(BF)
    g_eg = ((g_ug - g_unit * jnp.sum(g_unit * g_ug, axis=-1, keepdims=True)) * g_inv).astype(BF)
    for k, (pool, grad, dest) in enumerate(((s_pool, s_eg, gs_hbm), (g_pool, g_eg, gg_hbm))):
        for p in range(2):
            half = pl.ds(p * (C // 2), C // 2)
            buf[k, half] = lax.dot_general(pool[:, p * (C // 2):(p + 1) * (C // 2)], grad, (((0,), (0,)), ((), ())),
                                           preferred_element_type=F32)
            cp = pltpu.make_async_copy(buf.at[k, half], dest.at[half], sem.at[2 * k + p])
            cp.start()
            outs.append(cp)
    loss_ref[0] = jnp.sum(jnp.where(row == mine[0], losses, 0.0))
    for cp in outs:
        cp.wait()


def head(mine, sharp, tot, sproj, gproj, o, oe):
    return pl.pallas_call(
        head_kernel,
        name="contrastive_head",
        out_shape=(jax.ShapeDtypeStruct((1,), F32), jax.ShapeDtypeStruct((C, E), F32),
                   jax.ShapeDtypeStruct((C, E), F32), jax.ShapeDtypeStruct((2, 1, ROWS, COLS, C), F32)),
        in_specs=[SM, SM] + [VM] * 5,
        out_specs=(SM, HBM, HBM, HBM),
        scratch_shapes=[pltpu.VMEM((2, C, E), F32), pltpu.SemaphoreType.DMA((4,)), pltpu.SemaphoreType.DMA((6,))],
        compiler_params=pltpu.CompilerParams(vmem_limit_bytes=16 * MIB),
    )(mine, sharp, tot, sproj, gproj, o, oe)


def shards(state_maps, goal_maps, conv_one, conv_two, state_proj, goal_proj, inv_temp, pair_index):
    strips, batch = lax.axis_size("strip"), lax.axis_size("batch")
    mine = lax.axis_index("batch").astype(jnp.int32)
    here = jnp.stack([lax.axis_index("strip").astype(jnp.int32), jnp.int32(strips), pair_index[0]])
    w1 = conv_one.reshape(3, 3 * C, C)
    w2 = conv_two.reshape(3, 3 * C, C)
    chip, cross = pack(here, state_maps, goal_maps)
    chip = lax.ppermute(chip, "strip", [(i, i ^ 1) for i in range(strips)])
    cross = lax.ppermute(cross, "strip", [(i, i + 2 * (i % 2) - 1) for i in range(1, strips - 1)])
    x, xw, hw, o, sums, w1, w2 = interior(state_maps, goal_maps, w1, w2)
    oe, share, sp, gp = edges(here, chip, cross, x, xw, hw, sums, w1, w2, state_proj, goal_proj)
    share = lax.psum(share, "strip", axis_index_groups=[[2 * i, 2 * i + 1] for i in range(strips // 2)]).astype(BF)
    groups = [[b * strips + s for b in range(batch) for s in range(core, strips, 2)] for core in range(2)]
    copies = jnp.broadcast_to(share, (batch * strips // 2, *share.shape))
    got = lax.all_to_all(copies, ("batch", "strip"), 0, 0, tiled=True, axis_index_groups=groups)
    got = got.reshape(batch, strips // 2, 2, C + 128).astype(F32)
    tot = jnp.moveaxis(jnp.sum(got, axis=1), 1, 0)
    tot = tot * jnp.where(jnp.arange(C + 128) < C, 1.0, 1.0 / strips)
    return head(mine.reshape(1), inv_temp, tot, sp, gp, o, oe)


def solution(mesh):
    placed = (
        P("batch", "strip", None, None),
        P("batch", "strip", None, None),
        P(),
        P(),
        P(),
        P(),
        P(),
        P("batch"),
    )
    return jax.shard_map(
        shards,
        mesh=mesh,
        in_specs=placed,
        out_specs=(P("batch"), P(), P(), P(None, "batch", "strip", None, None)),
        check_vma=False,
    )
```

```python
import functools
import jax
import jax.numpy as jnp
from jax import lax
from jax.experimental import pallas as pl
from jax.experimental.pallas import tpu as pltpu
from jax.sharding import PartitionSpec as P

ROWS, COLS, C, E = 16, 64, 256, 1024
BF, F32 = jnp.bfloat16, jnp.float32
MIB = 1 << 20
HBM = pl.BlockSpec(memory_space=pltpu.MemorySpace.HBM)
VM = pl.BlockSpec(memory_space=pltpu.MemorySpace.VMEM)
SM = pl.BlockSpec(memory_space=pltpu.MemorySpace.SMEM)


def in_hbm(*arrays):
    return [pltpu.with_memory_space_constraint(a, pltpu.MemorySpace.HBM) for a in arrays]


def pack_kernel(here, s_hbm, g_hbm, chip, cross, sems):
    odd = lax.rem(here[0], 2)
    copies = []
    for f, ref in enumerate((s_hbm, g_hbm)):
        tail = (ROWS - 2) * (1 - odd)
        head = (ROWS - 2) * odd
        copies.append(pltpu.make_async_copy(ref.at[0, pl.ds(tail, 2)], chip.at[f], sems.at[f]))
        copies.append(pltpu.make_async_copy(ref.at[0, pl.ds(head, 2)], cross.at[f], sems.at[2 + f]))
    for cp in copies:
        cp.start()
    for cp in copies:
        cp.wait()


def pack(here, s, g):
    side = jax.ShapeDtypeStruct((2, 2, COLS, C), BF)
    return pl.pallas_call(
        pack_kernel,
        name="pack_halo_rows",
        out_shape=(side, side),
        in_specs=[SM, HBM, HBM],
        out_specs=(VM, VM),
        scratch_shapes=[pltpu.SemaphoreType.DMA((4,))],
        compiler_params=pltpu.CompilerParams(vmem_limit_bytes=2 * MIB),
    )(here, *in_hbm(s, g))


def widen(row):
    col = lax.broadcasted_iota(jnp.int32, row.shape, 0)
    left = jnp.where(col == 0, 0.0, pltpu.roll(row, 1, 0))
    right = jnp.where(col == COLS - 1, 0.0, pltpu.roll(row, COLS - 1, 0))
    return jnp.concatenate([left.astype(BF), row.astype(BF), right.astype(BF)], axis=-1)


def conv(wide, first, rows, weights):
    total = None
    for dy in range(3):
        lhs = wide[pl.ds(first + dy, rows)].reshape(rows * COLS, 3 * C)
        part = jnp.dot(lhs, weights[dy], preferred_element_type=F32)
        total = part if total is None else total + part
    return total


def conv_of(rows, weights):
    total = None
    for dy in range(3):
        lhs = jnp.concatenate([rows[dy], rows[dy + 1]], axis=0)
        part = jnp.dot(lhs, weights[dy], preferred_element_type=F32)
        total = part if total is None else total + part
    return total


def spans(total, step):
    return [(r, min(step, total - r)) for r in range(0, total, step)]


def interior_kernel(step1, step2, s_hbm, g_hbm, w1_hbm, w2_hbm, x, xw, hw, o, sum_ref, w1, w2, sems):
    cx = [[pltpu.make_async_copy(ref.at[0, pl.ds(8 * p, 8)], x.at[f, pl.ds(8 * p, 8)], sems.at[2 * f + p])
           for p in range(2)] for f, ref in enumerate((s_hbm, g_hbm))]
    cw1 = pltpu.make_async_copy(w1_hbm, w1, sems.at[4])
    cw2 = pltpu.make_async_copy(w2_hbm, w2, sems.at[5])
    cx[0][0].start(); cw1.start(); cx[0][1].start(); cw2.start(); cx[1][0].start(); cx[1][1].start()

    def spread(f, rows):
        for r in rows:
            xw[f, r] = widen(jnp.maximum(x[f, r].astype(F32), 0.0))

    def first(f, r, n):
        h = jnp.maximum(conv(xw.at[f], r, n, w1), 0.0)
        for k in range(n):
            hw[f, r + k] = widen(h[k * COLS:(k + 1) * COLS])

    def second(f, r, n, acc):
        y = conv(hw.at[f], r, n, w2)
        y = jnp.maximum(y + x[f, r + 2:r + 2 + n].reshape(n * COLS, C).astype(F32), 0.0)
        o[f, r:r + n] = y.reshape(n, COLS, C)
        part = jnp.sum(y.reshape(n * COLS // 8, 8, C), axis=0)
        return part if acc is None else acc + part

    cx[0][0].wait()
    spread(0, range(8))
    cx[0][1].wait()
    spread(0, range(8, 16))
    cw1.wait()
    for r, n in spans(14, step1):
        first(0, r, n)
    cx[1][0].wait(); cx[1][1].wait(); cw2.wait()
    acc = None
    todo = list(range(16))
    plan = spans(12, step2)
    for i, (r, n) in enumerate(plan):
        share = todo[i * 16 // len(plan):(i + 1) * 16 // len(plan)]
        spread(1, share)
        acc = second(0, r, n, acc)
    sum_ref[0] = acc
    for r, n in spans(14, step1):
        first(1, r, n)
    acc = None
    for r, n in spans(12, step2):
        acc = second(1, r, n, acc)
    sum_ref[1] = acc


def interior(s, g, w1, w2, step1=7, step2=6):
    wide = jax.ShapeDtypeStruct((3, 3 * C, C), BF)
    return pl.pallas_call(
        functools.partial(interior_kernel, step1, step2),
        name="interior_rows",
        out_shape=(jax.ShapeDtypeStruct((2, ROWS, COLS, C), BF),
                   jax.ShapeDtypeStruct((2, ROWS, COLS, 3 * C), BF),
                   jax.ShapeDtypeStruct((2, 14, COLS, 3 * C), BF),
                   jax.ShapeDtypeStruct((2, 12, COLS, C), F32),
                   jax.ShapeDtypeStruct((2, 8, C), F32), wide, wide),
        in_specs=[HBM] * 4,
        out_specs=(VM,) * 7,
        scratch_shapes=[pltpu.SemaphoreType.DMA((6,))],
        compiler_params=pltpu.CompilerParams(vmem_limit_bytes=24 * MIB),
        cost_estimate=pl.CostEstimate(flops=4_200_000_000, transcendentals=0, bytes_accessed=6_000_000),
    )(*in_hbm(s, g, w1, w2))


def edge_kernel(here, chip, cross, x, xw, hw, sums, w1, w2, sp_hbm, gp_hbm, o, share, sp, gp, halo, hh, sems):
    csp = pltpu.make_async_copy(sp_hbm, sp, sems.at[0])
    cgp = pltpu.make_async_copy(gp_hbm, gp, sems.at[1])
    csp.start(); cgp.start()
    odd = lax.rem(here[0], 2)
    for f in range(2):
        for r in range(2):
            a = widen(jnp.maximum(chip[f, r].astype(F32), 0.0))
            b = widen(jnp.maximum(cross[f, r].astype(F32), 0.0))
            halo[2 * f + 1 - odd, r] = a
            halo[2 * f + odd, r] = b
    for k in range(4):
        f = k // 2
        if k % 2 == 0:
            rows = [halo[k, 0], halo[k, 1], xw[f, 0], xw[f, 1]]
        else:
            rows = [xw[f, ROWS - 2], xw[f, ROWS - 1], halo[k, 0], halo[k, 1]]
        h = jnp.maximum(conv_of(rows, w1), 0.0)
        for r in range(2):
            row = h[r * COLS:(r + 1) * COLS]
            if k % 2 == 0 and r == 0:
                row = jnp.where(here[0] > 0, row, 0.0)
            if k % 2 == 1 and r == 1:
                row = jnp.where(here[0] < here[1] - 1, row, 0.0)
            hh[k, r] = widen(row)
    tot = [sums[0], sums[1]]
    for k in range(4):
        f = k // 2
        if k % 2 == 0:
            rows = [hh[k, 0], hh[k, 1], hw[f, 0], hw[f, 1]]
        else:
            rows = [hw[f, 12], hw[f, 13], hh[k, 0], hh[k, 1]]
        y = conv_of(rows, w2)
        y = jnp.maximum(y + x[f, 14 * (k % 2):14 * (k % 2) + 2].reshape(2 * COLS, C).astype(F32), 0.0)
        o[k] = y.reshape(2, COLS, C)
        tot[f] = tot[f] + jnp.sum(y.reshape(16, 8, C), axis=0)
    scale = 1.0 / (here[1] * (ROWS * COLS)).astype(F32)
    for f in range(2):
        share[f:f + 1, :C] = jnp.sum(tot[f], axis=0, keepdims=True) * scale
    share[:, C:] = jnp.full((2, 128), here[2], jnp.int32).astype(F32)
    csp.wait(); cgp.wait()


def edges(here, chip, cross, x, xw, hw, sums, w1, w2, sp, gp):
    proj = jax.ShapeDtypeStruct((C, E), BF)
    return pl.pallas_call(
        edge_kernel,
        name="edge_rows",
        out_shape=(jax.ShapeDtypeStruct((4, 2, COLS, C), F32), jax.ShapeDtypeStruct((2, C + 128), F32), proj, proj),
        in_specs=[SM] + [VM] * 8 + [HBM] * 2,
        out_specs=(VM,) * 4,
        scratch_shapes=[
            pltpu.VMEM((4, 2, COLS, 3 * C), BF),
            pltpu.VMEM((4, 2, COLS, 3 * C), BF),
            pltpu.SemaphoreType.DMA((2,)),
        ],
        compiler_params=pltpu.CompilerParams(vmem_limit_bytes=24 * MIB),
        cost_estimate=pl.CostEstimate(flops=1_200_000_000, transcendentals=0, bytes_accessed=4_000_000),
    )(here, chip, cross, x, xw, hw, sums, w1, w2, *in_hbm(sp, gp))


def head_kernel(mine, sharp, tot, sproj, gproj, o, oe, loss_ref, gs_hbm, gg_hbm, out_hbm, buf, sem, osem):
    outs = []
    for f in range(2):
        outs.append(pltpu.make_async_copy(o.at[f], out_hbm.at[f, 0, pl.ds(2, 12)], osem.at[3 * f]))
        for k in range(2):
            outs.append(pltpu.make_async_copy(oe.at[2 * f + k], out_hbm.at[f, 0, pl.ds(14 * k, 2)], osem.at[3 * f + 1 + k]))
    for cp in outs:
        cp.start()
    pairs = tot.shape[1]
    s_pool = tot[0, :, :C].astype(BF)
    g_pool = tot[1, :, :C].astype(BF)
    label = tot[0, :, C:C + 1]
    temp = sharp[0]
    s_emb = jnp.dot(s_pool, sproj[...], preferred_element_type=F32)
    g_emb = jnp.dot(g_pool, gproj[...], preferred_element_type=F32)
    s_inv = lax.rsqrt(jnp.sum(s_emb * s_emb, axis=-1, keepdims=True) + 1e-06)
    g_inv = lax.rsqrt(jnp.sum(g_emb * g_emb, axis=-1, keepdims=True) + 1e-06)
    s_unit = s_emb * s_inv
    g_unit = g_emb * g_inv
    s_bf = s_unit.astype(BF)
    g_bf = g_unit.astype(BF)
    logits = temp * lax.dot_general(s_bf, g_bf, (((1,), (1,)), ((), ())), preferred_element_type=F32)
    ex = jnp.exp(logits)
    row_total = jnp.sum(ex, axis=1, keepdims=True)
    column = lax.broadcasted_iota(jnp.int32, (pairs, pairs), 1).astype(F32)
    matched = column == label
    positive = jnp.sum(jnp.where(matched, logits, 0.0), axis=1, keepdims=True)
    losses = jnp.log(row_total) - positive
    row = lax.broadcasted_iota(jnp.int32, (pairs, 1), 0)
    lgrad = (ex / row_total - jnp.where(matched, 1.0, 0.0)).astype(BF)
    s_ug = temp * jnp.dot(lgrad, g_bf, preferred_element_type=F32)
    g_ug = temp * lax.dot_general(lgrad, s_bf, (((0,), (0,)), ((), ())), preferred_element_type=F32)
    s_eg = ((s_ug - s_unit * jnp.sum(s_unit * s_ug, axis=-1, keepdims=True)) * s_inv).astype(BF)
    g_eg = ((g_ug - g_unit * jnp.sum(g_unit * g_ug, axis=-1, keepdims=True)) * g_inv).astype(BF)
    for k, (pool, grad, dest) in enumerate(((s_pool, s_eg, gs_hbm), (g_pool, g_eg, gg_hbm))):
        for p in range(2):
            half = pl.ds(p * (C // 2), C // 2)
            buf[k, half] = lax.dot_general(pool[:, p * (C // 2):(p + 1) * (C // 2)], grad, (((0,), (0,)), ((), ())),
                                           preferred_element_type=F32)
            cp = pltpu.make_async_copy(buf.at[k, half], dest.at[half], sem.at[2 * k + p])
            cp.start()
            outs.append(cp)
    loss_ref[0] = jnp.sum(jnp.where(row == mine[0], losses, 0.0))
    for cp in outs:
        cp.wait()


def head(mine, sharp, tot, sproj, gproj, o, oe):
    return pl.pallas_call(
        head_kernel,
        name="contrastive_head",
        out_shape=(jax.ShapeDtypeStruct((1,), F32), jax.ShapeDtypeStruct((C, E), F32),
                   jax.ShapeDtypeStruct((C, E), F32), jax.ShapeDtypeStruct((2, 1, ROWS, COLS, C), F32)),
        in_specs=[SM, SM] + [VM] * 5,
        out_specs=(SM, HBM, HBM, HBM),
        scratch_shapes=[pltpu.VMEM((2, C, E), F32), pltpu.SemaphoreType.DMA((4,)), pltpu.SemaphoreType.DMA((6,))],
        compiler_params=pltpu.CompilerParams(vmem_limit_bytes=16 * MIB),
    )(mine, sharp, tot, sproj, gproj, o, oe)


def shards(state_maps, goal_maps, conv_one, conv_two, state_proj, goal_proj, inv_temp, pair_index):
    strips, batch = lax.axis_size("strip"), lax.axis_size("batch")
    mine = lax.axis_index("batch").astype(jnp.int32)
    here = jnp.stack([lax.axis_index("strip").astype(jnp.int32), jnp.int32(strips), pair_index[0]])
    w1 = conv_one.reshape(3, 3 * C, C)
    w2 = conv_two.reshape(3, 3 * C, C)
    chip, cross = pack(here, state_maps, goal_maps)
    chip = lax.ppermute(chip, "strip", [(i, i ^ 1) for i in range(strips)])
    cross = lax.ppermute(cross, "strip", [(i, i + 2 * (i % 2) - 1) for i in range(1, strips - 1)])
    x, xw, hw, o, sums, w1, w2 = interior(state_maps, goal_maps, w1, w2)
    oe, share, sp, gp = edges(here, chip, cross, x, xw, hw, sums, w1, w2, state_proj, goal_proj)
    share = lax.psum(share, "strip", axis_index_groups=[[2 * i, 2 * i + 1] for i in range(strips // 2)]).astype(BF)
    groups = [[b * strips + s for b in range(batch) for s in range(core, strips, 2)] for core in range(2)]
    copies = jnp.broadcast_to(share, (batch * strips // 2, *share.shape))
    got = lax.all_to_all(copies, ("batch", "strip"), 0, 0, tiled=True, axis_index_groups=groups)
    got = got.reshape(batch, strips // 2, 2, C + 128).astype(F32)
    tot = jnp.moveaxis(jnp.sum(got, axis=1), 1, 0)
    tot = tot * jnp.where(jnp.arange(C + 128) < C, 1.0, 1.0 / strips)
    return head(mine.reshape(1), inv_temp, tot, sp, gp, o, oe)


def solution(mesh):
    placed = (
        P("batch", "strip", None, None),
        P("batch", "strip", None, None),
        P(),
        P(),
        P(),
        P(),
        P(),
        P("batch"),
    )
    return jax.shard_map(
        shards,
        mesh=mesh,
        in_specs=placed,
        out_specs=(P("batch"), P(), P(), P(None, "batch", "strip", None, None)),
        check_vma=False,
    )
```

```python
import functools
import jax
import jax.numpy as jnp
from jax import lax
from jax.experimental import pallas as pl
from jax.experimental.pallas import tpu as pltpu
from jax.sharding import PartitionSpec as P

ROWS, COLS, C, E = 16, 64, 256, 1024
BF, F32 = jnp.bfloat16, jnp.float32
MIB = 1 << 20
HBM = pl.BlockSpec(memory_space=pltpu.MemorySpace.HBM)
VM = pl.BlockSpec(memory_space=pltpu.MemorySpace.VMEM)
SM = pl.BlockSpec(memory_space=pltpu.MemorySpace.SMEM)


def in_hbm(*arrays):
    return [pltpu.with_memory_space_constraint(a, pltpu.MemorySpace.HBM) for a in arrays]


def load_kernel(s_hbm, g_hbm, w1_hbm, chip, cross, x, w1, sems):
    odd = lax.rem(lax.axis_index("strip"), 2)
    copies = []
    for f, ref in enumerate((s_hbm, g_hbm)):
        tail = (ROWS - 2) * (1 - odd)
        head = (ROWS - 2) * odd
        copies.append((ref.at[0, pl.ds(tail, 2)], chip.at[f]))
        copies.append((ref.at[0, pl.ds(head, 2)], cross.at[f]))
    for f, ref in enumerate((s_hbm, g_hbm)):
        copies.append((ref.at[0], x.at[f]))
    for dy in range(3):
        copies.append((w1_hbm.at[dy], w1.at[dy]))
    copies = [pltpu.make_async_copy(a, b, sems.at[k]) for k, (a, b) in enumerate(copies)]
    for cp in copies:
        cp.start()
    for cp in copies:
        cp.wait()


def load(s, g, w1):
    side = jax.ShapeDtypeStruct((2, 2, COLS, C), BF)
    return pl.pallas_call(
        load_kernel,
        name="load_rows",
        out_shape=(side, side, jax.ShapeDtypeStruct((2, ROWS, COLS, C), BF), jax.ShapeDtypeStruct(w1.shape, BF)),
        in_specs=[HBM] * 3,
        out_specs=(VM,) * 4,
        scratch_shapes=[pltpu.SemaphoreType.DMA((9,))],
        compiler_params=pltpu.CompilerParams(vmem_limit_bytes=8 * MIB),
    )(*in_hbm(s, g, w1))


def widen(row):
    col = lax.broadcasted_iota(jnp.int32, row.shape, 0)
    left = jnp.where(col == 0, 0.0, pltpu.roll(row, 1, 0))
    right = jnp.where(col == COLS - 1, 0.0, pltpu.roll(row, COLS - 1, 0))
    return jnp.concatenate([left.astype(BF), row.astype(BF), right.astype(BF)], axis=-1)


def conv(wide, first, rows, weights):
    total = None
    for dy in range(3):
        lhs = wide[pl.ds(first + dy, rows)].reshape(rows * COLS, 3 * C)
        part = jnp.dot(lhs, weights[dy], preferred_element_type=F32)
        total = part if total is None else total + part
    return total


def conv_of(rows, weights):
    total = None
    for dy in range(3):
        lhs = jnp.concatenate([rows[dy], rows[dy + 1]], axis=0)
        part = jnp.dot(lhs, weights[dy], preferred_element_type=F32)
        total = part if total is None else total + part
    return total


def spans(total, step):
    return [(r, min(step, total - r)) for r in range(0, total, step)]


def interior_kernel(step1, step2, x, w1, w2_hbm, sp_hbm, gp_hbm, xw, hw, o, sum_ref, w2, sp, gp, sems):
    cw2 = pltpu.make_async_copy(w2_hbm, w2, sems.at[0])
    csp = pltpu.make_async_copy(sp_hbm, sp, sems.at[1])
    cgp = pltpu.make_async_copy(gp_hbm, gp, sems.at[2])
    cw2.start(); csp.start(); cgp.start()

    def spread(f, rows):
        for r in rows:
            xw[f, r] = widen(jnp.maximum(x[f, r].astype(F32), 0.0))

    def first(f, r, n):
        h = jnp.maximum(conv(xw.at[f], r, n, w1), 0.0)
        for k in range(n):
            hw[f, r + k] = widen(h[k * COLS:(k + 1) * COLS])

    def second(f, r, n, acc):
        y = conv(hw.at[f], r, n, w2)
        y = jnp.maximum(y + x[f, r + 2:r + 2 + n].reshape(n * COLS, C).astype(F32), 0.0)
        o[f, r:r + n] = y.reshape(n, COLS, C)
        part = jnp.sum(y.reshape(n * COLS // 8, 8, C), axis=0)
        return part if acc is None else acc + part

    spread(0, range(step1 + 2))
    plan = spans(14, step1)
    done = step1 + 2
    for i, (r, n) in enumerate(plan):
        if i + 1 < len(plan):
            upto = plan[i + 1][0] + plan[i + 1][1] + 2
            spread(0, range(done, upto))
            done = upto
        first(0, r, n)
    cw2.wait()
    acc = None
    plan = spans(12, step2)
    for i, (r, n) in enumerate(plan):
        spread(1, range(i * 16 // len(plan), (i + 1) * 16 // len(plan)))
        acc = second(0, r, n, acc)
    sum_ref[0] = acc
    for r, n in spans(14, step1):
        first(1, r, n)
    acc = None
    for r, n in spans(12, step2):
        acc = second(1, r, n, acc)
    sum_ref[1] = acc
    csp.wait(); cgp.wait()


def interior(x, w1, w2, sp, gp, step1=7, step2=6):
    proj = jax.ShapeDtypeStruct((C, E), BF)
    return pl.pallas_call(
        functools.partial(interior_kernel, step1, step2),
        name="interior_rows",
        out_shape=(jax.ShapeDtypeStruct((2, ROWS, COLS, 3 * C), BF),
                   jax.ShapeDtypeStruct((2, 14, COLS, 3 * C), BF),
                   jax.ShapeDtypeStruct((2, 12, COLS, C), F32),
                   jax.ShapeDtypeStruct((2, 8, C), F32), jax.ShapeDtypeStruct(w2.shape, BF), proj, proj),
        in_specs=[VM] * 2 + [HBM] * 3,
        out_specs=(VM,) * 7,
        scratch_shapes=[pltpu.SemaphoreType.DMA((3,))],
        compiler_params=pltpu.CompilerParams(vmem_limit_bytes=24 * MIB),
        cost_estimate=pl.CostEstimate(flops=4_200_000_000, transcendentals=0, bytes_accessed=6_000_000),
    )(x, w1, *in_hbm(w2, sp, gp))


def edge_kernel(label, chip, cross, x, xw, hw, sums, w1, w2, o, copies, halo, hh):
    here, strips = lax.axis_index("strip"), lax.axis_size("strip")
    odd = lax.rem(here, 2)
    for f in range(2):
        for r in range(2):
            halo[2 * f + 1 - odd, r] = widen(jnp.maximum(chip[f, r].astype(F32), 0.0))
            halo[2 * f + odd, r] = widen(jnp.maximum(cross[f, r].astype(F32), 0.0))
    for k in range(4):
        f = k // 2
        if k % 2 == 0:
            rows = [halo[k, 0], halo[k, 1], xw[f, 0], xw[f, 1]]
        else:
            rows = [xw[f, ROWS - 2], xw[f, ROWS - 1], halo[k, 0], halo[k, 1]]
        h = jnp.maximum(conv_of(rows, w1), 0.0)
        for r in range(2):
            row = h[r * COLS:(r + 1) * COLS]
            if k % 2 == 0 and r == 0:
                row = jnp.where(here > 0, row, 0.0)
            if k % 2 == 1 and r == 1:
                row = jnp.where(here < strips - 1, row, 0.0)
            hh[k, r] = widen(row)
    tot = [sums[0], sums[1]]
    for k in range(4):
        f = k // 2
        if k % 2 == 0:
            rows = [hh[k, 0], hh[k, 1], hw[f, 0], hw[f, 1]]
        else:
            rows = [hw[f, 12], hw[f, 13], hh[k, 0], hh[k, 1]]
        y = conv_of(rows, w2)
        y = jnp.maximum(y + x[f, 14 * (k % 2):14 * (k % 2) + 2].reshape(2 * COLS, C).astype(F32), 0.0)
        o[k] = y.reshape(2, COLS, C)
        tot[f] = tot[f] + jnp.sum(y.reshape(16, 8, C), axis=0)
    scale = 1.0 / (strips * ROWS * COLS)
    mark = jnp.full((1, 128), label[0], jnp.int32).astype(F32) * (1.0 / strips)
    for f in range(2):
        row = jnp.concatenate([jnp.sum(tot[f], axis=0, keepdims=True) * scale, mark], axis=1)
        for n in range(copies.shape[0]):
            copies[n, f:f + 1] = row


def edges(label, chip, cross, x, xw, hw, sums, w1, w2, members):
    return pl.pallas_call(
        edge_kernel,
        name="edge_rows",
        out_shape=(jax.ShapeDtypeStruct((4, 2, COLS, C), F32), jax.ShapeDtypeStruct((members, 2, C + 128), F32)),
        in_specs=[SM] + [VM] * 8,
        out_specs=(VM,) * 2,
        scratch_shapes=[
            pltpu.VMEM((4, 2, COLS, 3 * C), BF),
            pltpu.VMEM((4, 2, COLS, 3 * C), BF),
        ],
        compiler_params=pltpu.CompilerParams(vmem_limit_bytes=24 * MIB),
        cost_estimate=pl.CostEstimate(flops=1_200_000_000, transcendentals=0, bytes_accessed=4_000_000),
    )(label, chip, cross, x, xw, hw, sums, w1, w2)


def write_kernel(o, oe, out_hbm, sems):
    outs = []
    for f in range(2):
        outs.append(pltpu.make_async_copy(o.at[f], out_hbm.at[f, 0, pl.ds(2, 12)], sems.at[3 * f]))
        for k in range(2):
            outs.append(pltpu.make_async_copy(oe.at[2 * f + k], out_hbm.at[f, 0, pl.ds(14 * k, 2)], sems.at[3 * f + 1 + k]))
    for cp in outs:
        cp.start()
    for cp in outs:
        cp.wait()


def write(o, oe):
    return pl.pallas_call(
        write_kernel,
        name="write_maps",
        out_shape=jax.ShapeDtypeStruct((2, 1, ROWS, COLS, C), F32),
        in_specs=[VM] * 2,
        out_specs=HBM,
        scratch_shapes=[pltpu.SemaphoreType.DMA((6,))],
        compiler_params=pltpu.CompilerParams(vmem_limit_bytes=2 * MIB),
        cost_estimate=pl.CostEstimate(flops=0, transcendentals=0, bytes_accessed=4_000_000),
    )(o, oe)


def head_kernel(sharp, tot, sproj, gproj, loss_ref, gs_hbm, gg_hbm, buf, sem):
    pairs = tot.shape[1]
    s_pool = tot[0, :, :C].astype(BF)
    g_pool = tot[1, :, :C].astype(BF)
    label = tot[0, :, C:C + 1]
    temp = sharp[0]
    s_emb = jnp.dot(s_pool, sproj[...], preferred_element_type=F32)
    g_emb = jnp.dot(g_pool, gproj[...], preferred_element_type=F32)
    s_inv = lax.rsqrt(jnp.sum(s_emb * s_emb, axis=-1, keepdims=True) + 1e-06)
    g_inv = lax.rsqrt(jnp.sum(g_emb * g_emb, axis=-1, keepdims=True) + 1e-06)
    s_unit = s_emb * s_inv
    g_unit = g_emb * g_inv
    s_bf = s_unit.astype(BF)
    g_bf = g_unit.astype(BF)
    logits = temp * lax.dot_general(s_bf, g_bf, (((1,), (1,)), ((), ())), preferred_element_type=F32)
    ex = jnp.exp(logits)
    row_total = jnp.sum(ex, axis=1, keepdims=True)
    column = lax.broadcasted_iota(jnp.int32, (pairs, pairs), 1).astype(F32)
    matched = column == label
    positive = jnp.sum(jnp.where(matched, logits, 0.0), axis=1, keepdims=True)
    losses = jnp.log(row_total) - positive
    row = lax.broadcasted_iota(jnp.int32, (pairs, 1), 0)
    lgrad = (ex / row_total - jnp.where(matched, 1.0, 0.0)).astype(BF)
    s_ug = temp * jnp.dot(lgrad, g_bf, preferred_element_type=F32)
    g_ug = temp * lax.dot_general(lgrad, s_bf, (((0,), (0,)), ((), ())), preferred_element_type=F32)
    s_eg = ((s_ug - s_unit * jnp.sum(s_unit * s_ug, axis=-1, keepdims=True)) * s_inv).astype(BF)
    g_eg = ((g_ug - g_unit * jnp.sum(g_unit * g_ug, axis=-1, keepdims=True)) * g_inv).astype(BF)
    outs = []
    for k, (pool, grad, dest) in enumerate(((s_pool, s_eg, gs_hbm), (g_pool, g_eg, gg_hbm))):
        for p in range(2):
            half = pl.ds(p * (C // 2), C // 2)
            buf[k, half] = lax.dot_general(pool[:, p * (C // 2):(p + 1) * (C // 2)], grad, (((0,), (0,)), ((), ())),
                                           preferred_element_type=F32)
            cp = pltpu.make_async_copy(buf.at[k, half], dest.at[half], sem.at[2 * k + p])
            cp.start()
            outs.append(cp)
    loss_ref[0] = jnp.sum(jnp.where(row == lax.axis_index("batch"), losses, 0.0))
    for cp in outs:
        cp.wait()


def head(sharp, tot, sproj, gproj):
    return pl.pallas_call(
        head_kernel,
        name="contrastive_head",
        out_shape=(jax.ShapeDtypeStruct((1,), F32), jax.ShapeDtypeStruct((C, E), F32),
                   jax.ShapeDtypeStruct((C, E), F32)),
        in_specs=[SM] + [VM] * 3,
        out_specs=(SM, HBM, HBM),
        scratch_shapes=[pltpu.VMEM((2, C, E), F32), pltpu.SemaphoreType.DMA((4,))],
        compiler_params=pltpu.CompilerParams(vmem_limit_bytes=16 * MIB),
    )(sharp, tot, sproj, gproj)


def gather_groups(batch, strips, inner):
    lines = {}
    for b in range(batch):
        for s in range(strips):
            half, plane = divmod(b, batch // 2)
            lines.setdefault(plane if inner else (half, s), []).append(b * strips + s)
    return list(lines.values())


def shards(state_maps, goal_maps, conv_one, conv_two, state_proj, goal_proj, inv_temp, pair_index):
    strips, batch = lax.axis_size("strip"), lax.axis_size("batch")
    w1 = conv_one.reshape(3, 3 * C, C)
    w2 = conv_two.reshape(3, 3 * C, C)
    chip, cross, x, w1 = load(state_maps, goal_maps, w1)
    chip = lax.ppermute(chip, "strip", [(i, i ^ 1) for i in range(strips)])
    cross = lax.ppermute(cross, "strip", [(i, i + 2 * (i % 2) - 1) for i in range(1, strips - 1)])
    xw, hw, o, sums, w2, sp, gp = interior(x, w1, w2, state_proj, goal_proj)
    oe, copies = edges(pair_index, chip, cross, x, xw, hw, sums, w1, w2, 2 * strips)
    both = ("batch", "strip")
    line = lax.all_to_all(copies, both, 0, 0, tiled=True, axis_index_groups=gather_groups(batch, strips, True))
    means = jnp.sum(line.reshape(2, strips, 2, C + 128), axis=1).astype(BF).reshape(4, C + 128)
    copies = jnp.broadcast_to(means, (batch // 2, 4, C + 128))
    got = lax.all_to_all(copies, both, 0, 0, tiled=True, axis_index_groups=gather_groups(batch, strips, False))
    tot = jnp.transpose(got.reshape(batch // 2, 2, 2, C + 128).astype(F32), (2, 1, 0, 3)).reshape(2, batch, C + 128)
    out = write(o, oe)
    loss, gs, gg = head(inv_temp, tot, sp, gp)
    return loss, gs, gg, out


def solution(mesh):
    placed = (
        P("batch", "strip", None, None),
        P("batch", "strip", None, None),
        P(),
        P(),
        P(),
        P(),
        P(),
        P("batch"),
    )
    return jax.shard_map(
        shards,
        mesh=mesh,
        in_specs=placed,
        out_specs=(P("batch"), P(), P(), P(None, "batch", "strip", None, None)),
        check_vma=False,
    )
```

```python
import functools
import jax
import jax.numpy as jnp
from jax import lax
from jax.experimental import pallas as pl
from jax.experimental.pallas import tpu as pltpu
from jax.sharding import PartitionSpec as P

ROWS, COLS, C, E = 16, 64, 256, 1024
BF, F32 = jnp.bfloat16, jnp.float32
MIB = 1 << 20
HBM = pl.BlockSpec(memory_space=pltpu.MemorySpace.HBM)
VM = pl.BlockSpec(memory_space=pltpu.MemorySpace.VMEM)
SM = pl.BlockSpec(memory_space=pltpu.MemorySpace.SMEM)


def in_hbm(*arrays):
    return [pltpu.with_memory_space_constraint(a, pltpu.MemorySpace.HBM) for a in arrays]


def pack_kernel(s_hbm, g_hbm, cross, sems):
    odd = lax.rem(lax.axis_index("strip"), 2)
    copies = [pltpu.make_async_copy(ref.at[0, pl.ds((ROWS - 2) * odd, 2)], cross.at[f], sems.at[f])
              for f, ref in enumerate((s_hbm, g_hbm))]
    for cp in copies:
        cp.start()
    for cp in copies:
        cp.wait()


def pack(s, g):
    return pl.pallas_call(
        pack_kernel,
        name="pack_rows",
        out_shape=jax.ShapeDtypeStruct((2, 2, COLS, C), BF),
        in_specs=[HBM] * 2,
        out_specs=VM,
        scratch_shapes=[pltpu.SemaphoreType.DMA((2,))],
        compiler_params=pltpu.CompilerParams(vmem_limit_bytes=2 * MIB),
    )(*in_hbm(s, g))


def load_kernel(s_hbm, g_hbm, w1_hbm, packed, chip, x, w1, sems):
    odd = lax.rem(lax.axis_index("strip"), 2)
    copies = [(ref.at[0, pl.ds((ROWS - 2) * (1 - odd), 2)], chip.at[f]) for f, ref in enumerate((s_hbm, g_hbm))]
    copies += [(ref.at[0], x.at[f]) for f, ref in enumerate((s_hbm, g_hbm))]
    copies += [(w1_hbm.at[dy], w1.at[dy]) for dy in range(3)]
    copies = [pltpu.make_async_copy(a, b, sems.at[k]) for k, (a, b) in enumerate(copies)]
    for cp in copies:
        cp.start()
    for cp in copies:
        cp.wait()


def load(s, g, w1, packed):
    return pl.pallas_call(
        load_kernel,
        name="load_rows",
        out_shape=(jax.ShapeDtypeStruct((2, 2, COLS, C), BF), jax.ShapeDtypeStruct((2, ROWS, COLS, C), BF),
                   jax.ShapeDtypeStruct(w1.shape, BF)),
        in_specs=[HBM] * 3 + [VM],
        out_specs=(VM,) * 3,
        scratch_shapes=[pltpu.SemaphoreType.DMA((7,))],
        compiler_params=pltpu.CompilerParams(vmem_limit_bytes=8 * MIB),
    )(*in_hbm(s, g, w1), packed)


def widen(row):
    col = lax.broadcasted_iota(jnp.int32, row.shape, 0)
    left = jnp.where(col == 0, 0.0, pltpu.roll(row, 1, 0))
    right = jnp.where(col == COLS - 1, 0.0, pltpu.roll(row, COLS - 1, 0))
    return jnp.concatenate([left.astype(BF), row.astype(BF), right.astype(BF)], axis=-1)


def conv(wide, first, rows, weights):
    total = None
    for dy in range(3):
        lhs = wide[pl.ds(first + dy, rows)].reshape(rows * COLS, 3 * C)
        part = jnp.dot(lhs, weights[dy], preferred_element_type=F32)
        total = part if total is None else total + part
    return total


def conv_of(rows, weights):
    total = None
    for dy in range(3):
        lhs = jnp.concatenate([rows[dy], rows[dy + 1]], axis=0)
        part = jnp.dot(lhs, weights[dy], preferred_element_type=F32)
        total = part if total is None else total + part
    return total


def spans(total, step):
    return [(r, min(step, total - r)) for r in range(0, total, step)]


def interior_kernel(step1, step2, x, w1, w2_hbm, sp_hbm, gp_hbm, xw, hw, o, sum_ref, w2, sp, gp, sems):
    cw2 = pltpu.make_async_copy(w2_hbm, w2, sems.at[0])
    csp = pltpu.make_async_copy(sp_hbm, sp, sems.at[1])
    cgp = pltpu.make_async_copy(gp_hbm, gp, sems.at[2])
    cw2.start(); csp.start(); cgp.start()

    def spread(f, rows):
        for r in rows:
            xw[f, r] = widen(jnp.maximum(x[f, r].astype(F32), 0.0))

    def first(f, r, n):
        h = jnp.maximum(conv(xw.at[f], r, n, w1), 0.0)
        for k in range(n):
            hw[f, r + k] = widen(h[k * COLS:(k + 1) * COLS])

    def second(f, r, n, acc):
        y = conv(hw.at[f], r, n, w2)
        y = jnp.maximum(y + x[f, r + 2:r + 2 + n].reshape(n * COLS, C).astype(F32), 0.0)
        o[f, r:r + n] = y.reshape(n, COLS, C)
        part = jnp.sum(y.reshape(n * COLS // 8, 8, C), axis=0)
        return part if acc is None else acc + part

    spread(0, range(step1 + 2))
    plan = spans(14, step1)
    done = step1 + 2
    for i, (r, n) in enumerate(plan):
        if i + 1 < len(plan):
            upto = plan[i + 1][0] + plan[i + 1][1] + 2
            spread(0, range(done, upto))
            done = upto
        first(0, r, n)
    cw2.wait()
    acc = None
    plan = spans(12, step2)
    for i, (r, n) in enumerate(plan):
        spread(1, range(i * 16 // len(plan), (i + 1) * 16 // len(plan)))
        acc = second(0, r, n, acc)
    sum_ref[0] = acc
    for r, n in spans(14, step1):
        first(1, r, n)
    acc = None
    for r, n in spans(12, step2):
        acc = second(1, r, n, acc)
    sum_ref[1] = acc
    csp.wait(); cgp.wait()


def interior(x, w1, w2, sp, gp, step1=7, step2=4):
    proj = jax.ShapeDtypeStruct((C, E), BF)
    return pl.pallas_call(
        functools.partial(interior_kernel, step1, step2),
        name="interior_rows",
        out_shape=(jax.ShapeDtypeStruct((2, ROWS, COLS, 3 * C), BF),
                   jax.ShapeDtypeStruct((2, 14, COLS, 3 * C), BF),
                   jax.ShapeDtypeStruct((2, 12, COLS, C), F32),
                   jax.ShapeDtypeStruct((2, 8, C), F32), jax.ShapeDtypeStruct(w2.shape, BF), proj, proj),
        in_specs=[VM] * 2 + [HBM] * 3,
        out_specs=(VM,) * 7,
        scratch_shapes=[pltpu.SemaphoreType.DMA((3,))],
        compiler_params=pltpu.CompilerParams(vmem_limit_bytes=24 * MIB),
        cost_estimate=pl.CostEstimate(flops=4_200_000_000, transcendentals=0, bytes_accessed=6_000_000),
    )(x, w1, *in_hbm(w2, sp, gp))


def edge_kernel(label, chip, cross, x, xw, hw, sums, w1, w2, inner, o, copies, out_hbm, halo, hh, sems):
    outs = [pltpu.make_async_copy(inner.at[f], out_hbm.at[f, 0, pl.ds(2, ROWS - 4)], sems.at[f]) for f in range(2)]
    for cp in outs:
        cp.start()
    here, strips = lax.axis_index("strip"), lax.axis_size("strip")
    odd = lax.rem(here, 2)
    for f in range(2):
        for r in range(2):
            halo[2 * f + 1 - odd, r] = widen(jnp.maximum(chip[f, r].astype(F32), 0.0))
            halo[2 * f + odd, r] = widen(jnp.maximum(cross[f, r].astype(F32), 0.0))
    for k in range(4):
        f = k // 2
        if k % 2 == 0:
            rows = [halo[k, 0], halo[k, 1], xw[f, 0], xw[f, 1]]
        else:
            rows = [xw[f, ROWS - 2], xw[f, ROWS - 1], halo[k, 0], halo[k, 1]]
        h = jnp.maximum(conv_of(rows, w1), 0.0)
        for r in range(2):
            row = h[r * COLS:(r + 1) * COLS]
            if k % 2 == 0 and r == 0:
                row = jnp.where(here > 0, row, 0.0)
            if k % 2 == 1 and r == 1:
                row = jnp.where(here < strips - 1, row, 0.0)
            hh[k, r] = widen(row)
    tot = [sums[0], sums[1]]
    for k in range(4):
        f = k // 2
        if k % 2 == 0:
            rows = [hh[k, 0], hh[k, 1], hw[f, 0], hw[f, 1]]
        else:
            rows = [hw[f, 12], hw[f, 13], hh[k, 0], hh[k, 1]]
        y = conv_of(rows, w2)
        y = jnp.maximum(y + x[f, 14 * (k % 2):14 * (k % 2) + 2].reshape(2 * COLS, C).astype(F32), 0.0)
        o[k] = y.reshape(2, COLS, C)
        tot[f] = tot[f] + jnp.sum(y.reshape(16, 8, C), axis=0)
    scale = 1.0 / (strips * ROWS * COLS)
    mark = jnp.broadcast_to(label[...].astype(F32) * (1.0 / strips), (1, 128))
    for f in range(2):
        row = jnp.concatenate([jnp.sum(tot[f], axis=0, keepdims=True) * scale, mark], axis=1)
        for n in range(copies.shape[0]):
            copies[n, f:f + 1] = row
    for cp in outs:
        cp.wait()


def edges(label, chip, cross, x, xw, hw, sums, w1, w2, inner, members):
    return pl.pallas_call(
        edge_kernel,
        name="edge_rows",
        out_shape=(jax.ShapeDtypeStruct((4, 2, COLS, C), F32), jax.ShapeDtypeStruct((members, 2, C + 128), F32),
                   jax.ShapeDtypeStruct((2, 1, ROWS, COLS, C), F32)),
        in_specs=[VM] * 10,
        out_specs=(VM, VM, HBM),
        scratch_shapes=[
            pltpu.VMEM((4, 2, COLS, 3 * C), BF),
            pltpu.VMEM((4, 2, COLS, 3 * C), BF),
            pltpu.SemaphoreType.DMA((2,)),
        ],
        compiler_params=pltpu.CompilerParams(vmem_limit_bytes=24 * MIB),
        cost_estimate=pl.CostEstimate(flops=1_200_000_000, transcendentals=0, bytes_accessed=4_000_000),
    )(label, chip, cross, x, xw, hw, sums, w1, w2, inner)


def head_kernel(sharp, tot, sproj, gproj, oe, partial_hbm, loss_ref, gs_hbm, gg_hbm, out_hbm, buf, sem, osem):
    outs = []
    for k in range(4):
        outs.append(pltpu.make_async_copy(oe.at[k], out_hbm.at[k // 2, 0, pl.ds((ROWS - 2) * (k % 2), 2)], osem.at[k]))
        outs[-1].start()
    pairs = tot.shape[1]
    s_pool = tot[0, :, :C].astype(BF)
    g_pool = tot[1, :, :C].astype(BF)
    label = tot[0, :, C:C + 1]
    temp = sharp[...]
    s_emb = jnp.dot(s_pool, sproj[...], preferred_element_type=F32)
    g_emb = jnp.dot(g_pool, gproj[...], preferred_element_type=F32)
    s_inv = lax.rsqrt(jnp.sum(s_emb * s_emb, axis=-1, keepdims=True) + 1e-06)
    g_inv = lax.rsqrt(jnp.sum(g_emb * g_emb, axis=-1, keepdims=True) + 1e-06)
    s_unit = s_emb * s_inv
    g_unit = g_emb * g_inv
    s_bf = s_unit.astype(BF)
    g_bf = g_unit.astype(BF)
    logits = temp * lax.dot_general(s_bf, g_bf, (((1,), (1,)), ((), ())), preferred_element_type=F32)
    ex = jnp.exp(logits)
    row_total = jnp.sum(ex, axis=1, keepdims=True)
    column = lax.broadcasted_iota(jnp.int32, (pairs, pairs), 1).astype(F32)
    matched = column == label
    lgrad = (ex / row_total - jnp.where(matched, 1.0, 0.0)).astype(BF)

    def finish(k, unit_grad, unit, inverse, pool, dest):
        grad = ((unit_grad - unit * jnp.sum(unit * unit_grad, axis=-1, keepdims=True)) * inverse).astype(BF)
        for p in range(2):
            half = pl.ds(p * (C // 2), C // 2)
            buf[k, half] = lax.dot_general(pool[:, p * (C // 2):(p + 1) * (C // 2)], grad, (((0,), (0,)), ((), ())),
                                           preferred_element_type=F32)
            cp = pltpu.make_async_copy(buf.at[k, half], dest.at[half], sem.at[2 * k + p])
            cp.start()
            outs.append(cp)

    s_ug = temp * jnp.dot(lgrad, g_bf, preferred_element_type=F32)
    finish(0, s_ug, s_unit, s_inv, s_pool, gs_hbm)
    g_ug = temp * lax.dot_general(lgrad, s_bf, (((0,), (0,)), ((), ())), preferred_element_type=F32)
    finish(1, g_ug, g_unit, g_inv, g_pool, gg_hbm)
    positive = jnp.sum(jnp.where(matched, logits, 0.0), axis=1, keepdims=True)
    losses = jnp.log(row_total) - positive
    row = lax.broadcasted_iota(jnp.int32, (pairs, 1), 0)
    loss_ref[0] = jnp.sum(jnp.where(row == lax.axis_index("batch"), losses, 0.0))
    for cp in outs:
        cp.wait()


def head(sharp, tot, sproj, gproj, oe, out):
    return pl.pallas_call(
        head_kernel,
        name="contrastive_head",
        out_shape=(jax.ShapeDtypeStruct((1,), F32), jax.ShapeDtypeStruct((C, E), F32),
                   jax.ShapeDtypeStruct((C, E), F32), jax.ShapeDtypeStruct(out.shape, F32)),
        in_specs=[VM] * 5 + [HBM],
        out_specs=(SM, HBM, HBM, HBM),
        input_output_aliases={5: 3},
        scratch_shapes=[pltpu.VMEM((2, C, E), F32), pltpu.SemaphoreType.DMA((4,)), pltpu.SemaphoreType.DMA((4,))],
        compiler_params=pltpu.CompilerParams(vmem_limit_bytes=16 * MIB),
    )(sharp, tot, sproj, gproj, oe, out)


def gather_groups(batch, strips, inner):
    lines = {}
    for b in range(batch):
        for s in range(strips):
            half, plane = divmod(b, batch // 2)
            lines.setdefault(plane if inner else (half, s), []).append(b * strips + s)
    return list(lines.values())


def shards(state_maps, goal_maps, conv_one, conv_two, state_proj, goal_proj, inv_temp, pair_index):
    strips, batch = lax.axis_size("strip"), lax.axis_size("batch")
    w1 = conv_one.reshape(3, 3 * C, C)
    w2 = conv_two.reshape(3, 3 * C, C)
    cross = pack(state_maps, goal_maps)
    chip, x, w1 = load(state_maps, goal_maps, w1, cross)
    cross = lax.ppermute(cross, "strip", [(i, i + 2 * (i % 2) - 1) for i in range(1, strips - 1)])
    chip = lax.ppermute(chip, "strip", [(i, i ^ 1) for i in range(strips)])
    xw, hw, inner, sums, w2, sp, gp = interior(x, w1, w2, state_proj, goal_proj)
    label = pair_index.reshape(1, 1)
    oe, copies, out = edges(label, chip, cross, x, xw, hw, sums, w1, w2, inner, 2 * strips)
    both = ("batch", "strip")
    line = lax.all_to_all(copies, both, 0, 0, tiled=True, axis_index_groups=gather_groups(batch, strips, True))
    means = jnp.sum(line.reshape(2, strips, 2, C + 128), axis=1).astype(BF).reshape(4, C + 128)
    copies = jnp.broadcast_to(means, (batch // 2, 4, C + 128))
    got = lax.all_to_all(copies, both, 0, 0, tiled=True, axis_index_groups=gather_groups(batch, strips, False))
    tot = jnp.transpose(got.reshape(batch // 2, 2, 2, C + 128).astype(F32), (2, 1, 0, 3)).reshape(2, batch, C + 128)
    return head(inv_temp.reshape(1, 1), tot, sp, gp, oe, out)


def solution(mesh):
    placed = (
        P("batch", "strip", None, None),
        P("batch", "strip", None, None),
        P(),
        P(),
        P(),
        P(),
        P(),
        P("batch"),
    )
    return jax.shard_map(
        shards,
        mesh=mesh,
        in_specs=placed,
        out_specs=(P("batch"), P(), P(), P(None, "batch", "strip", None, None)),
        check_vma=False,
    )
```

```python
import functools
import jax
import jax.numpy as jnp
from jax import lax
from jax.experimental import pallas as pl
from jax.experimental.pallas import tpu as pltpu
from jax.sharding import PartitionSpec as P

ROWS, COLS, C, E = 16, 64, 256, 1024
BF, F32 = jnp.bfloat16, jnp.float32
MIB = 1 << 20
HBM = pl.BlockSpec(memory_space=pltpu.MemorySpace.HBM)
VM = pl.BlockSpec(memory_space=pltpu.MemorySpace.VMEM)
SM = pl.BlockSpec(memory_space=pltpu.MemorySpace.SMEM)


def in_hbm(*arrays):
    return [pltpu.with_memory_space_constraint(a, pltpu.MemorySpace.HBM) for a in arrays]


def load_kernel(s_hbm, g_hbm, w1_hbm, cross, chip, x, w1, sems):
    odd = lax.rem(lax.axis_index("strip"), 2)
    copies = []
    for f, ref in enumerate((s_hbm, g_hbm)):
        tail = (ROWS - 2) * (1 - odd)
        head = (ROWS - 2) * odd
        copies.append((ref.at[0, pl.ds(tail, 2)], chip.at[f]))
        copies.append((ref.at[0, pl.ds(head, 2)], cross.at[f]))
    copies.append((s_hbm.at[0], x.at[0]))
    for dy in range(3):
        copies.append((w1_hbm.at[dy], w1.at[dy]))
    copies = [pltpu.make_async_copy(a, b, sems.at[k]) for k, (a, b) in enumerate(copies)]
    for cp in copies:
        cp.start()
    for cp in copies:
        cp.wait()


def load(s, g, w1):
    side = jax.ShapeDtypeStruct((2, 2, COLS, C), BF)
    return pl.pallas_call(
        load_kernel,
        name="load_rows",
        out_shape=(side, side, jax.ShapeDtypeStruct((1, ROWS, COLS, C), BF), jax.ShapeDtypeStruct(w1.shape, BF)),
        in_specs=[HBM] * 3,
        out_specs=(VM,) * 4,
        scratch_shapes=[pltpu.SemaphoreType.DMA((8,))],
        compiler_params=pltpu.CompilerParams(vmem_limit_bytes=8 * MIB),
    )(*in_hbm(s, g, w1))


def widen(row):
    col = lax.broadcasted_iota(jnp.int32, row.shape, 0)
    left = jnp.where(col == 0, 0.0, pltpu.roll(row, 1, 0))
    right = jnp.where(col == COLS - 1, 0.0, pltpu.roll(row, COLS - 1, 0))
    return jnp.concatenate([left.astype(BF), row.astype(BF), right.astype(BF)], axis=-1)


def conv(wide, first, rows, weights):
    total = None
    for dy in range(3):
        lhs = wide[pl.ds(first + dy, rows)].reshape(rows * COLS, 3 * C)
        part = jnp.dot(lhs, weights[dy], preferred_element_type=F32)
        total = part if total is None else total + part
    return total


def conv_of(rows, weights):
    total = None
    for dy in range(3):
        lhs = jnp.concatenate([rows[dy], rows[dy + 1]], axis=0)
        part = jnp.dot(lhs, weights[dy], preferred_element_type=F32)
        total = part if total is None else total + part
    return total


def spans(total, step):
    return [(r, min(step, total - r)) for r in range(0, total, step)]


def interior_kernel(step1, step2, x0, w1, g_hbm, w2_hbm, sp_hbm, gp_hbm, xw, hw, o, sum_ref, x1, w2, sp, gp, sems):
    cw2 = pltpu.make_async_copy(w2_hbm, w2, sems.at[0])
    csp = pltpu.make_async_copy(sp_hbm, sp, sems.at[1])
    cgp = pltpu.make_async_copy(gp_hbm, gp, sems.at[2])
    cx1 = pltpu.make_async_copy(g_hbm.at[0], x1.at[0], sems.at[3])
    cw2.start(); cx1.start(); csp.start(); cgp.start()
    x = (x0.at[0], x1.at[0])

    def spread(f, rows):
        for r in rows:
            xw[f, r] = widen(jnp.maximum(x[f][r].astype(F32), 0.0))

    def first(f, r, n):
        h = jnp.maximum(conv(xw.at[f], r, n, w1), 0.0)
        for k in range(n):
            hw[f, r + k] = widen(h[k * COLS:(k + 1) * COLS])

    def second(f, r, n, acc):
        y = conv(hw.at[f], r, n, w2)
        y = jnp.maximum(y + x[f][r + 2:r + 2 + n].reshape(n * COLS, C).astype(F32), 0.0)
        o[f, r:r + n] = y.reshape(n, COLS, C)
        part = jnp.sum(y.reshape(n * COLS // 8, 8, C), axis=0)
        return part if acc is None else acc + part

    spread(0, range(step1 + 2))
    plan = spans(14, step1)
    done = step1 + 2
    for i, (r, n) in enumerate(plan):
        if i + 1 < len(plan):
            upto = plan[i + 1][0] + plan[i + 1][1] + 2
            spread(0, range(done, upto))
            done = upto
        first(0, r, n)
    cw2.wait(); cx1.wait()
    acc = None
    plan = spans(12, step2)
    for i, (r, n) in enumerate(plan):
        spread(1, range(i * 16 // len(plan), (i + 1) * 16 // len(plan)))
        acc = second(0, r, n, acc)
    sum_ref[0] = acc
    for r, n in spans(14, step1):
        first(1, r, n)
    acc = None
    for r, n in spans(12, step2):
        acc = second(1, r, n, acc)
    sum_ref[1] = acc
    csp.wait(); cgp.wait()


def interior(x0, w1, g, w2, sp, gp, step1=7, step2=4):
    proj = jax.ShapeDtypeStruct((C, E), BF)
    return pl.pallas_call(
        functools.partial(interior_kernel, step1, step2),
        name="interior_rows",
        out_shape=(jax.ShapeDtypeStruct((2, ROWS, COLS, 3 * C), BF),
                   jax.ShapeDtypeStruct((2, 14, COLS, 3 * C), BF),
                   jax.ShapeDtypeStruct((2, 12, COLS, C), F32),
                   jax.ShapeDtypeStruct((2, 8, C), F32), jax.ShapeDtypeStruct(x0.shape, BF),
                   jax.ShapeDtypeStruct(w2.shape, BF), proj, proj),
        in_specs=[VM] * 2 + [HBM] * 4,
        out_specs=(VM,) * 8,
        scratch_shapes=[pltpu.SemaphoreType.DMA((4,))],
        compiler_params=pltpu.CompilerParams(vmem_limit_bytes=24 * MIB),
        cost_estimate=pl.CostEstimate(flops=4_200_000_000, transcendentals=0, bytes_accessed=6_000_000),
    )(x0, w1, *in_hbm(g, w2, sp, gp))


def edge_kernel(label, cross, chip, x0, x1, xw, hw, sums, w1, w2, o, copies, halo, hh):
    here, strips = lax.axis_index("strip"), lax.axis_size("strip")
    odd = lax.rem(here, 2)
    for f in range(2):
        for r in range(2):
            halo[2 * f + 1 - odd, r] = widen(jnp.maximum(chip[f, r].astype(F32), 0.0))
            halo[2 * f + odd, r] = widen(jnp.maximum(cross[f, r].astype(F32), 0.0))
    for k in range(4):
        f = k // 2
        if k % 2 == 0:
            rows = [halo[k, 0], halo[k, 1], xw[f, 0], xw[f, 1]]
        else:
            rows = [xw[f, ROWS - 2], xw[f, ROWS - 1], halo[k, 0], halo[k, 1]]
        h = jnp.maximum(conv_of(rows, w1), 0.0)
        for r in range(2):
            row = h[r * COLS:(r + 1) * COLS]
            if k % 2 == 0 and r == 0:
                row = jnp.where(here > 0, row, 0.0)
            if k % 2 == 1 and r == 1:
                row = jnp.where(here < strips - 1, row, 0.0)
            hh[k, r] = widen(row)
    tot = [sums[0], sums[1]]
    for k in range(4):
        f = k // 2
        if k % 2 == 0:
            rows = [hh[k, 0], hh[k, 1], hw[f, 0], hw[f, 1]]
        else:
            rows = [hw[f, 12], hw[f, 13], hh[k, 0], hh[k, 1]]
        y = conv_of(rows, w2)
        y = jnp.maximum(y + (x0, x1)[f][0, 14 * (k % 2):14 * (k % 2) + 2].reshape(2 * COLS, C).astype(F32), 0.0)
        o[k] = y.reshape(2, COLS, C)
        tot[f] = tot[f] + jnp.sum(y.reshape(16, 8, C), axis=0)
    scale = 1.0 / (strips * ROWS * COLS)
    mark = jnp.full((1, 128), label[0], jnp.int32).astype(F32) * (1.0 / strips)
    for f in range(2):
        row = jnp.concatenate([jnp.sum(tot[f], axis=0, keepdims=True) * scale, mark], axis=1)
        for n in range(copies.shape[0]):
            copies[n, f:f + 1] = row


def edges(label, chip, cross, x0, x1, xw, hw, sums, w1, w2, members):
    return pl.pallas_call(
        edge_kernel,
        name="edge_rows",
        out_shape=(jax.ShapeDtypeStruct((4, 2, COLS, C), F32), jax.ShapeDtypeStruct((members, 2, C + 128), F32)),
        in_specs=[SM] + [VM] * 9,
        out_specs=(VM,) * 2,
        scratch_shapes=[
            pltpu.VMEM((4, 2, COLS, 3 * C), BF),
            pltpu.VMEM((4, 2, COLS, 3 * C), BF),
        ],
        compiler_params=pltpu.CompilerParams(vmem_limit_bytes=24 * MIB),
        cost_estimate=pl.CostEstimate(flops=1_200_000_000, transcendentals=0, bytes_accessed=4_000_000),
    )(label, cross, chip, x0, x1, xw, hw, sums, w1, w2)


def write_kernel(o, oe, out_hbm, sems):
    outs = []
    for f in range(2):
        outs.append(pltpu.make_async_copy(o.at[f], out_hbm.at[f, 0, pl.ds(2, 12)], sems.at[3 * f]))
        for k in range(2):
            outs.append(pltpu.make_async_copy(oe.at[2 * f + k], out_hbm.at[f, 0, pl.ds(14 * k, 2)], sems.at[3 * f + 1 + k]))
    for cp in outs:
        cp.start()
    for cp in outs:
        cp.wait()


def write(o, oe):
    return pl.pallas_call(
        write_kernel,
        name="write_maps",
        out_shape=jax.ShapeDtypeStruct((2, 1, ROWS, COLS, C), F32),
        in_specs=[VM] * 2,
        out_specs=HBM,
        scratch_shapes=[pltpu.SemaphoreType.DMA((6,))],
        compiler_params=pltpu.CompilerParams(vmem_limit_bytes=2 * MIB),
        cost_estimate=pl.CostEstimate(flops=0, transcendentals=0, bytes_accessed=4_000_000),
    )(o, oe)


def head_kernel(sharp, tot, sproj, gproj, loss_ref, gs_hbm, gg_hbm, buf, sem):
    pairs = tot.shape[1]
    s_pool = tot[0, :, :C].astype(BF)
    g_pool = tot[1, :, :C].astype(BF)
    label = tot[0, :, C:C + 1]
    temp = sharp[0]
    s_emb = jnp.dot(s_pool, sproj[...], preferred_element_type=F32)
    g_emb = jnp.dot(g_pool, gproj[...], preferred_element_type=F32)
    s_inv = lax.rsqrt(jnp.sum(s_emb * s_emb, axis=-1, keepdims=True) + 1e-06)
    g_inv = lax.rsqrt(jnp.sum(g_emb * g_emb, axis=-1, keepdims=True) + 1e-06)
    s_unit = s_emb * s_inv
    g_unit = g_emb * g_inv
    s_bf = s_unit.astype(BF)
    g_bf = g_unit.astype(BF)
    logits = temp * lax.dot_general(s_bf, g_bf, (((1,), (1,)), ((), ())), preferred_element_type=F32)
    ex = jnp.exp(logits)
    row_total = jnp.sum(ex, axis=1, keepdims=True)
    column = lax.broadcasted_iota(jnp.int32, (pairs, pairs), 1).astype(F32)
    matched = column == label
    lgrad = (ex / row_total - jnp.where(matched, 1.0, 0.0)).astype(BF)

    outs = []

    def finish(k, unit_grad, unit, inverse, pool, dest):
        grad = ((unit_grad - unit * jnp.sum(unit * unit_grad, axis=-1, keepdims=True)) * inverse).astype(BF)
        for p in range(2):
            half = pl.ds(p * (C // 2), C // 2)
            buf[k, half] = lax.dot_general(pool[:, p * (C // 2):(p + 1) * (C // 2)], grad, (((0,), (0,)), ((), ())),
                                           preferred_element_type=F32)
            cp = pltpu.make_async_copy(buf.at[k, half], dest.at[half], sem.at[2 * k + p])
            cp.start()
            outs.append(cp)

    s_ug = temp * jnp.dot(lgrad, g_bf, preferred_element_type=F32)
    finish(0, s_ug, s_unit, s_inv, s_pool, gs_hbm)
    g_ug = temp * lax.dot_general(lgrad, s_bf, (((0,), (0,)), ((), ())), preferred_element_type=F32)
    finish(1, g_ug, g_unit, g_inv, g_pool, gg_hbm)
    positive = jnp.sum(jnp.where(matched, logits, 0.0), axis=1, keepdims=True)
    losses = jnp.log(row_total) - positive
    row = lax.broadcasted_iota(jnp.int32, (pairs, 1), 0)
    loss_ref[0] = jnp.sum(jnp.where(row == lax.axis_index("batch"), losses, 0.0))
    for cp in outs:
        cp.wait()


def head(sharp, tot, sproj, gproj):
    return pl.pallas_call(
        head_kernel,
        name="contrastive_head",
        out_shape=(jax.ShapeDtypeStruct((1,), F32), jax.ShapeDtypeStruct((C, E), F32),
                   jax.ShapeDtypeStruct((C, E), F32)),
        in_specs=[SM] + [VM] * 3,
        out_specs=(SM, HBM, HBM),
        scratch_shapes=[pltpu.VMEM((2, C, E), F32), pltpu.SemaphoreType.DMA((4,))],
        compiler_params=pltpu.CompilerParams(vmem_limit_bytes=16 * MIB),
    )(sharp, tot, sproj, gproj)


def gather_groups(batch, strips, inner):
    lines = {}
    for b in range(batch):
        for s in range(strips):
            half, plane = divmod(b, batch // 2)
            lines.setdefault(plane if inner else (half, s), []).append(b * strips + s)
    return list(lines.values())


def shards(state_maps, goal_maps, conv_one, conv_two, state_proj, goal_proj, inv_temp, pair_index):
    strips, batch = lax.axis_size("strip"), lax.axis_size("batch")
    w1 = conv_one.reshape(3, 3 * C, C)
    w2 = conv_two.reshape(3, 3 * C, C)
    cross, chip, x0, w1 = load(state_maps, goal_maps, w1)
    cross = lax.ppermute(cross, "strip", [(i, i + 2 * (i % 2) - 1) for i in range(1, strips - 1)])
    chip = lax.ppermute(chip, "strip", [(i, i ^ 1) for i in range(strips)])
    xw, hw, o, sums, x1, w2, sp, gp = interior(x0, w1, goal_maps, w2, state_proj, goal_proj)
    oe, copies = edges(pair_index, chip, cross, x0, x1, xw, hw, sums, w1, w2, 2 * strips)
    both = ("batch", "strip")
    line = lax.all_to_all(copies, both, 0, 0, tiled=True, axis_index_groups=gather_groups(batch, strips, True))
    means = jnp.sum(line.reshape(2, strips, 2, C + 128), axis=1).astype(BF).reshape(4, C + 128)
    copies = jnp.broadcast_to(means, (batch // 2, 4, C + 128))
    got = lax.all_to_all(copies, both, 0, 0, tiled=True, axis_index_groups=gather_groups(batch, strips, False))
    tot = jnp.transpose(got.reshape(batch // 2, 2, 2, C + 128).astype(F32), (2, 1, 0, 3)).reshape(2, batch, C + 128)
    out = write(o, oe)
    loss, gs, gg = head(inv_temp, tot, sp, gp)
    return loss, gs, gg, out


def solution(mesh):
    placed = (
        P("batch", "strip", None, None),
        P("batch", "strip", None, None),
        P(),
        P(),
        P(),
        P(),
        P(),
        P("batch"),
    )
    return jax.shard_map(
        shards,
        mesh=mesh,
        in_specs=placed,
        out_specs=(P("batch"), P(), P(), P(None, "batch", "strip", None, None)),
        check_vma=False,
    )
```

```python
import functools
import jax
import jax.numpy as jnp
from jax import lax
from jax.experimental import pallas as pl
from jax.experimental.pallas import tpu as pltpu
from jax.sharding import PartitionSpec as P

ROWS, COLS, C, E = 16, 64, 256, 1024
BF, F32 = jnp.bfloat16, jnp.float32
MIB = 1 << 20
HBM = pl.BlockSpec(memory_space=pltpu.MemorySpace.HBM)
VM = pl.BlockSpec(memory_space=pltpu.MemorySpace.VMEM)
SM = pl.BlockSpec(memory_space=pltpu.MemorySpace.SMEM)


def in_hbm(*arrays):
    return [pltpu.with_memory_space_constraint(a, pltpu.MemorySpace.HBM) for a in arrays]


def load_kernel(s_hbm, g_hbm, w1_hbm, cross, chip, x, w1, sems):
    odd = lax.rem(lax.axis_index("strip"), 2)
    copies = []
    for f, ref in enumerate((s_hbm, g_hbm)):
        tail = (ROWS - 2) * (1 - odd)
        head = (ROWS - 2) * odd
        copies.append((ref.at[0, pl.ds(tail, 2)], chip.at[f]))
        copies.append((ref.at[0, pl.ds(head, 2)], cross.at[f]))
    copies.append((s_hbm.at[0], x.at[0]))
    copies.append((w1_hbm.at[0], w1.at[0]))
    copies = [pltpu.make_async_copy(a, b, sems.at[k]) for k, (a, b) in enumerate(copies)]
    for cp in copies:
        cp.start()
    for cp in copies:
        cp.wait()


def load(s, g, w1):
    side = jax.ShapeDtypeStruct((2, 2, COLS, C), BF)
    return pl.pallas_call(
        load_kernel,
        name="load_rows",
        out_shape=(side, side, jax.ShapeDtypeStruct((1, ROWS, COLS, C), BF), jax.ShapeDtypeStruct((1, 3 * C, C), BF)),
        in_specs=[HBM] * 3,
        out_specs=(VM,) * 4,
        scratch_shapes=[pltpu.SemaphoreType.DMA((6,))],
        compiler_params=pltpu.CompilerParams(vmem_limit_bytes=8 * MIB),
    )(*in_hbm(s, g, w1))


def widen(row):
    col = lax.broadcasted_iota(jnp.int32, row.shape, 0)
    left = jnp.where(col == 0, 0.0, pltpu.roll(row, 1, 0))
    right = jnp.where(col == COLS - 1, 0.0, pltpu.roll(row, COLS - 1, 0))
    return jnp.concatenate([left.astype(BF), row.astype(BF), right.astype(BF)], axis=-1)


def conv(wide, first, rows, weights, waits=None):
    total = None
    for dy in range(3):
        if waits is not None and waits[dy] is not None:
            waits[dy].wait()
        lhs = wide[pl.ds(first + dy, rows)].reshape(rows * COLS, 3 * C)
        part = jnp.dot(lhs, weights[dy][...], preferred_element_type=F32)
        total = part if total is None else total + part
    return total


def conv_of(rows, weights):
    total = None
    for dy in range(3):
        lhs = jnp.concatenate([rows[dy], rows[dy + 1]], axis=0)
        part = jnp.dot(lhs, weights[dy][...], preferred_element_type=F32)
        total = part if total is None else total + part
    return total


def spans(total, step):
    return [(r, min(step, total - r)) for r in range(0, total, step)]


def interior_kernel(step1, step2, x0, w1a, label_hbm, sharp_hbm, w1_hbm, g_hbm, w2_hbm, sp_hbm, gp_hbm,
                    xw, hw, o, sum_ref, marks, x1, w1b, w2, sp, gp, label, sharp, sems):
    cw2 = pltpu.make_async_copy(w2_hbm, w2, sems.at[0])
    csp = pltpu.make_async_copy(sp_hbm, sp, sems.at[1])
    cgp = pltpu.make_async_copy(gp_hbm, gp, sems.at[2])
    cx1 = pltpu.make_async_copy(g_hbm.at[0], x1.at[0], sems.at[3])
    clabel = pltpu.make_async_copy(label_hbm, label, sems.at[4])
    csharp = pltpu.make_async_copy(sharp_hbm, sharp, sems.at[5])
    cw1 = [pltpu.make_async_copy(w1_hbm.at[dy], w1b.at[dy - 1], sems.at[5 + dy]) for dy in (1, 2)]
    cw1[0].start(); cw1[1].start(); cw2.start(); cx1.start(); csp.start(); cgp.start(); clabel.start(); csharp.start()
    x = (x0.at[0], x1.at[0])
    first_weights = [w1a.at[0], w1b.at[0], w1b.at[1]]
    second_weights = [w2.at[dy] for dy in range(3)]

    def spread(f, rows):
        for r in rows:
            xw[f, r] = widen(jnp.maximum(x[f][r].astype(F32), 0.0))

    def first(f, r, n, waits=None):
        h = jnp.maximum(conv(xw.at[f], r, n, first_weights, waits), 0.0)
        for k in range(n):
            hw[f, r + k] = widen(h[k * COLS:(k + 1) * COLS])

    def second(f, r, n, acc):
        y = conv(hw.at[f], r, n, second_weights)
        y = jnp.maximum(y + x[f][r + 2:r + 2 + n].reshape(n * COLS, C).astype(F32), 0.0)
        o[f, r:r + n] = y.reshape(n, COLS, C)
        part = jnp.sum(y.reshape(n * COLS // 8, 8, C), axis=0)
        return part if acc is None else acc + part

    spread(0, range(step1 + 2))
    plan = spans(14, step1)
    done = step1 + 2
    for i, (r, n) in enumerate(plan):
        if i + 1 < len(plan):
            upto = plan[i + 1][0] + plan[i + 1][1] + 2
            spread(0, range(done, upto))
            done = upto
        first(0, r, n, [None] + cw1 if i == 0 else None)
    cw2.wait(); cx1.wait()
    acc = None
    plan = spans(12, step2)
    for i, (r, n) in enumerate(plan):
        spread(1, range(i * 16 // len(plan), (i + 1) * 16 // len(plan)))
        acc = second(0, r, n, acc)
    sum_ref[0] = acc
    for r, n in spans(14, step1):
        first(1, r, n)
    acc = None
    for r, n in spans(12, step2):
        acc = second(1, r, n, acc)
    sum_ref[1] = acc
    clabel.wait(); csharp.wait()
    marks[0:8] = jnp.full((8, 128), label[0], jnp.int32).astype(F32)
    marks[8:16] = jnp.full((8, 128), sharp[0], F32)
    csp.wait(); cgp.wait()


def interior(x0, w1a, label, sharp, w1, g, w2, sp, gp, step1=7, step2=4):
    proj = jax.ShapeDtypeStruct((C, E), BF)
    return pl.pallas_call(
        functools.partial(interior_kernel, step1, step2),
        name="interior_rows",
        out_shape=(jax.ShapeDtypeStruct((2, ROWS, COLS, 3 * C), BF),
                   jax.ShapeDtypeStruct((2, 14, COLS, 3 * C), BF),
                   jax.ShapeDtypeStruct((2, 12, COLS, C), F32),
                   jax.ShapeDtypeStruct((2, 8, C), F32), jax.ShapeDtypeStruct((16, 128), F32), jax.ShapeDtypeStruct(x0.shape, BF),
                   jax.ShapeDtypeStruct((2, 3 * C, C), BF), jax.ShapeDtypeStruct(w2.shape, BF), proj, proj),
        in_specs=[VM] * 2 + [HBM] * 7,
        out_specs=(VM,) * 10,
        scratch_shapes=[pltpu.SMEM((1,), jnp.int32), pltpu.SMEM((1,), F32), pltpu.SemaphoreType.DMA((8,))],
        compiler_params=pltpu.CompilerParams(vmem_limit_bytes=24 * MIB),
        cost_estimate=pl.CostEstimate(flops=4_200_000_000, transcendentals=0, bytes_accessed=6_000_000),
    )(x0, w1a, label, sharp, *in_hbm(w1, g, w2, sp, gp))


def edge_kernel(marks, cross, chip, x0, x1, xw, hw, sums, w1a, w1b, w2, inner, o, copies, out_hbm, halo, hh, sems):
    outs = [pltpu.make_async_copy(inner.at[f], out_hbm.at[f, 0, pl.ds(2, ROWS - 4)], sems.at[f]) for f in range(2)]
    for cp in outs:
        cp.start()
    w1 = [w1a.at[0], w1b.at[0], w1b.at[1]]
    w2 = [w2.at[dy] for dy in range(3)]
    here, strips = lax.axis_index("strip"), lax.axis_size("strip")
    odd = lax.rem(here, 2)
    for f in range(2):
        for r in range(2):
            halo[2 * f + 1 - odd, r] = widen(jnp.maximum(chip[f, r].astype(F32), 0.0))
            halo[2 * f + odd, r] = widen(jnp.maximum(cross[f, r].astype(F32), 0.0))
    for k in range(4):
        f = k // 2
        if k % 2 == 0:
            rows = [halo[k, 0], halo[k, 1], xw[f, 0], xw[f, 1]]
        else:
            rows = [xw[f, ROWS - 2], xw[f, ROWS - 1], halo[k, 0], halo[k, 1]]
        h = jnp.maximum(conv_of(rows, w1), 0.0)
        for r in range(2):
            row = h[r * COLS:(r + 1) * COLS]
            if k % 2 == 0 and r == 0:
                row = jnp.where(here > 0, row, 0.0)
            if k % 2 == 1 and r == 1:
                row = jnp.where(here < strips - 1, row, 0.0)
            hh[k, r] = widen(row)
    tot = [sums[0], sums[1]]
    for k in range(4):
        f = k // 2
        if k % 2 == 0:
            rows = [hh[k, 0], hh[k, 1], hw[f, 0], hw[f, 1]]
        else:
            rows = [hw[f, 12], hw[f, 13], hh[k, 0], hh[k, 1]]
        y = conv_of(rows, w2)
        y = jnp.maximum(y + (x0, x1)[f][0, 14 * (k % 2):14 * (k % 2) + 2].reshape(2 * COLS, C).astype(F32), 0.0)
        o[k] = y.reshape(2, COLS, C)
        tot[f] = tot[f] + jnp.sum(y.reshape(16, 8, C), axis=0)
    scale = 1.0 / (strips * ROWS * COLS)
    mark = marks[0:1] * (1.0 / strips)
    for f in range(2):
        row = jnp.concatenate([jnp.sum(tot[f], axis=0, keepdims=True) * scale, mark], axis=1)
        for n in range(copies.shape[0]):
            copies[n, f:f + 1] = row
    for cp in outs:
        cp.wait()


def edges(marks, cross, chip, x0, x1, xw, hw, sums, w1a, w1b, w2, inner, members):
    return pl.pallas_call(
        edge_kernel,
        name="edge_rows",
        out_shape=(jax.ShapeDtypeStruct((4, 2, COLS, C), F32), jax.ShapeDtypeStruct((members, 2, C + 128), F32),
                   jax.ShapeDtypeStruct((2, 1, ROWS, COLS, C), F32)),
        in_specs=[VM] * 12,
        out_specs=(VM, VM, HBM),
        scratch_shapes=[
            pltpu.VMEM((4, 2, COLS, 3 * C), BF),
            pltpu.VMEM((4, 2, COLS, 3 * C), BF),
            pltpu.SemaphoreType.DMA((2,)),
        ],
        compiler_params=pltpu.CompilerParams(vmem_limit_bytes=24 * MIB),
        cost_estimate=pl.CostEstimate(flops=1_200_000_000, transcendentals=0, bytes_accessed=4_000_000),
    )(marks, cross, chip, x0, x1, xw, hw, sums, w1a, w1b, w2, inner)


def head_kernel(marks, tot, sproj, gproj, oe, partial_hbm, loss_ref, gs_hbm, gg_hbm, out_hbm, buf, sem, osem):
    outs = []
    for k in range(4):
        outs.append(pltpu.make_async_copy(oe.at[k], out_hbm.at[k // 2, 0, pl.ds((ROWS - 2) * (k % 2), 2)], osem.at[k]))
        outs[-1].start()
    pairs = tot.shape[1]
    s_pool = tot[0, :, :C].astype(BF)
    g_pool = tot[1, :, :C].astype(BF)
    label = tot[0, :, C:C + 1]
    temp = marks[8:9, 0:1]
    s_emb = jnp.dot(s_pool, sproj[...], preferred_element_type=F32)
    g_emb = jnp.dot(g_pool, gproj[...], preferred_element_type=F32)
    s_inv = lax.rsqrt(jnp.sum(s_emb * s_emb, axis=-1, keepdims=True) + 1e-06)
    g_inv = lax.rsqrt(jnp.sum(g_emb * g_emb, axis=-1, keepdims=True) + 1e-06)
    s_unit = s_emb * s_inv
    g_unit = g_emb * g_inv
    s_bf = s_unit.astype(BF)
    g_bf = g_unit.astype(BF)
    logits = temp * lax.dot_general(s_bf, g_bf, (((1,), (1,)), ((), ())), preferred_element_type=F32)
    ex = jnp.exp(logits)
    row_total = jnp.sum(ex, axis=1, keepdims=True)
    column = lax.broadcasted_iota(jnp.int32, (pairs, pairs), 1).astype(F32)
    matched = column == label
    lgrad = (ex / row_total - jnp.where(matched, 1.0, 0.0)).astype(BF)

    def finish(k, unit_grad, unit, inverse, pool, dest):
        grad = ((unit_grad - unit * jnp.sum(unit * unit_grad, axis=-1, keepdims=True)) * inverse).astype(BF)
        for p in range(2):
            half = pl.ds(p * (C // 2), C // 2)
            buf[k, half] = lax.dot_general(pool[:, p * (C // 2):(p + 1) * (C // 2)], grad, (((0,), (0,)), ((), ())),
                                           preferred_element_type=F32)
            cp = pltpu.make_async_copy(buf.at[k, half], dest.at[half], sem.at[2 * k + p])
            cp.start()
            outs.append(cp)

    s_ug = temp * jnp.dot(lgrad, g_bf, preferred_element_type=F32)
    finish(0, s_ug, s_unit, s_inv, s_pool, gs_hbm)
    g_ug = temp * lax.dot_general(lgrad, s_bf, (((0,), (0,)), ((), ())), preferred_element_type=F32)
    finish(1, g_ug, g_unit, g_inv, g_pool, gg_hbm)
    positive = jnp.sum(jnp.where(matched, logits, 0.0), axis=1, keepdims=True)
    losses = jnp.log(row_total) - positive
    row = lax.broadcasted_iota(jnp.int32, (pairs, 1), 0)
    loss_ref[0] = jnp.sum(jnp.where(row == lax.axis_index("batch"), losses, 0.0))
    for cp in outs:
        cp.wait()


def head(marks, tot, sproj, gproj, oe, out):
    return pl.pallas_call(
        head_kernel,
        name="contrastive_head",
        out_shape=(jax.ShapeDtypeStruct((1,), F32), jax.ShapeDtypeStruct((C, E), F32),
                   jax.ShapeDtypeStruct((C, E), F32), jax.ShapeDtypeStruct(out.shape, F32)),
        in_specs=[VM] * 5 + [HBM],
        out_specs=(SM, HBM, HBM, HBM),
        input_output_aliases={5: 3},
        scratch_shapes=[pltpu.VMEM((2, C, E), F32), pltpu.SemaphoreType.DMA((4,)), pltpu.SemaphoreType.DMA((4,))],
        compiler_params=pltpu.CompilerParams(vmem_limit_bytes=16 * MIB),
    )(marks, tot, sproj, gproj, oe, out)


def gather_groups(batch, strips, inner):
    lines = {}
    for b in range(batch):
        for s in range(strips):
            half, plane = divmod(b, batch // 2)
            lines.setdefault(plane if inner else (half, s), []).append(b * strips + s)
    return list(lines.values())


def shards(state_maps, goal_maps, conv_one, conv_two, state_proj, goal_proj, inv_temp, pair_index):
    strips, batch = lax.axis_size("strip"), lax.axis_size("batch")
    w1 = conv_one.reshape(3, 3 * C, C)
    w2 = conv_two.reshape(3, 3 * C, C)
    cross, chip, x0, w1a = load(state_maps, goal_maps, w1)
    cross = lax.ppermute(cross, "strip", [(i, i + 2 * (i % 2) - 1) for i in range(1, strips - 1)])
    chip = lax.ppermute(chip, "strip", [(i, i ^ 1) for i in range(strips)])
    xw, hw, inner, sums, marks, x1, w1b, w2, sp, gp = interior(
        x0, w1a, pair_index, inv_temp, w1, goal_maps, w2, state_proj, goal_proj)
    oe, copies, out = edges(marks, cross, chip, x0, x1, xw, hw, sums, w1a, w1b, w2, inner, 2 * strips)
    both = ("batch", "strip")
    line = lax.all_to_all(copies, both, 0, 0, tiled=True, axis_index_groups=gather_groups(batch, strips, True))
    means = jnp.sum(line.reshape(2, strips, 2, C + 128), axis=1).astype(BF).reshape(4, C + 128)
    copies = jnp.broadcast_to(means, (batch // 2, 4, C + 128))
    got = lax.all_to_all(copies, both, 0, 0, tiled=True, axis_index_groups=gather_groups(batch, strips, False))
    tot = jnp.transpose(got.reshape(batch // 2, 2, 2, C + 128).astype(F32), (2, 1, 0, 3)).reshape(2, batch, C + 128)
    return head(marks, tot, sp, gp, oe, out)


def solution(mesh):
    placed = (
        P("batch", "strip", None, None),
        P("batch", "strip", None, None),
        P(),
        P(),
        P(),
        P(),
        P(),
        P("batch"),
    )
    return jax.shard_map(
        shards,
        mesh=mesh,
        in_specs=placed,
        out_specs=(P("batch"), P(), P(), P(None, "batch", "strip", None, None)),
        check_vma=False,
    )
```

```python
import functools
import jax
import jax.numpy as jnp
from jax import lax
from jax.experimental import pallas as pl
from jax.experimental.pallas import tpu as pltpu
from jax.sharding import PartitionSpec as P

ROWS, COLS, C, E = 16, 64, 256, 1024
BF, F32 = jnp.bfloat16, jnp.float32
MIB = 1 << 20
HBM = pl.BlockSpec(memory_space=pltpu.MemorySpace.HBM)
VM = pl.BlockSpec(memory_space=pltpu.MemorySpace.VMEM)
SM = pl.BlockSpec(memory_space=pltpu.MemorySpace.SMEM)


def in_hbm(*arrays):
    return [pltpu.with_memory_space_constraint(a, pltpu.MemorySpace.HBM) for a in arrays]


def load_kernel(s_hbm, g_hbm, w1_hbm, cross, chip, x, w1, sems):
    odd = lax.rem(lax.axis_index("strip"), 2)
    copies = []
    for f, ref in enumerate((s_hbm, g_hbm)):
        tail = (ROWS - 2) * (1 - odd)
        head = (ROWS - 2) * odd
        copies.append((ref.at[0, pl.ds(tail, 2)], chip.at[f]))
        copies.append((ref.at[0, pl.ds(head, 2)], cross.at[f]))
    copies.append((s_hbm.at[0], x.at[0]))
    for dy in range(3):
        copies.append((w1_hbm.at[dy], w1.at[dy]))
    copies = [pltpu.make_async_copy(a, b, sems.at[k]) for k, (a, b) in enumerate(copies)]
    for cp in copies:
        cp.start()
    for cp in copies:
        cp.wait()


def load(s, g, w1):
    side = jax.ShapeDtypeStruct((2, 2, COLS, C), BF)
    return pl.pallas_call(
        load_kernel,
        name="load_rows",
        out_shape=(side, side, jax.ShapeDtypeStruct((1, ROWS, COLS, C), BF), jax.ShapeDtypeStruct(w1.shape, BF)),
        in_specs=[HBM] * 3,
        out_specs=(VM,) * 4,
        scratch_shapes=[pltpu.SemaphoreType.DMA((8,))],
        compiler_params=pltpu.CompilerParams(vmem_limit_bytes=8 * MIB),
    )(*in_hbm(s, g, w1))


def widen(row):
    col = lax.broadcasted_iota(jnp.int32, row.shape, 0)
    left = jnp.where(col == 0, 0.0, pltpu.roll(row, 1, 0))
    right = jnp.where(col == COLS - 1, 0.0, pltpu.roll(row, COLS - 1, 0))
    return jnp.concatenate([left.astype(BF), row.astype(BF), right.astype(BF)], axis=-1)


def conv(wide, first, rows, weights):
    total = None
    for dy in range(3):
        lhs = wide[pl.ds(first + dy, rows)].reshape(rows * COLS, 3 * C)
        part = jnp.dot(lhs, weights[dy], preferred_element_type=F32)
        total = part if total is None else total + part
    return total


def conv_of(rows, weights):
    total = None
    for dy in range(3):
        lhs = jnp.concatenate([rows[dy], rows[dy + 1]], axis=0)
        part = jnp.dot(lhs, weights[dy], preferred_element_type=F32)
        total = part if total is None else total + part
    return total


def spans(total, step):
    return [(r, min(step, total - r)) for r in range(0, total, step)]


def interior_kernel(step1, step2, x0, w1, g_hbm, w2_hbm, sp_hbm, gp_hbm, xw, hw, o, sum_ref, x1, w2, sp, gp, sems):
    cw2 = pltpu.make_async_copy(w2_hbm, w2, sems.at[0])
    csp = pltpu.make_async_copy(sp_hbm, sp, sems.at[1])
    cgp = pltpu.make_async_copy(gp_hbm, gp, sems.at[2])
    cx1 = pltpu.make_async_copy(g_hbm.at[0], x1.at[0], sems.at[3])
    cw2.start(); cx1.start(); csp.start(); cgp.start()
    x = (x0.at[0], x1.at[0])

    def spread(f, rows):
        for r in rows:
            xw[f, r] = widen(jnp.maximum(x[f][r].astype(F32), 0.0))

    def first(f, r, n):
        h = jnp.maximum(conv(xw.at[f], r, n, w1), 0.0)
        for k in range(n):
            hw[f, r + k] = widen(h[k * COLS:(k + 1) * COLS])

    def second(f, r, n, acc):
        y = conv(hw.at[f], r, n, w2)
        y = jnp.maximum(y + x[f][r + 2:r + 2 + n].reshape(n * COLS, C).astype(F32), 0.0)
        o[f, r:r + n] = y.reshape(n, COLS, C)
        part = jnp.sum(y.reshape(n * COLS // 8, 8, C), axis=0)
        return part if acc is None else acc + part

    spread(0, range(step1 + 2))
    plan = spans(14, step1)
    done = step1 + 2
    for i, (r, n) in enumerate(plan):
        if i + 1 < len(plan):
            upto = plan[i + 1][0] + plan[i + 1][1] + 2
            spread(0, range(done, upto))
            done = upto
        first(0, r, n)
    cw2.wait(); cx1.wait()
    acc = None
    plan = spans(12, step2)
    for i, (r, n) in enumerate(plan):
        spread(1, range(i * 16 // len(plan), (i + 1) * 16 // len(plan)))
        acc = second(0, r, n, acc)
    sum_ref[0] = acc
    for r, n in spans(14, step1):
        first(1, r, n)
    acc = None
    for r, n in spans(12, step2):
        acc = second(1, r, n, acc)
    sum_ref[1] = acc
    csp.wait(); cgp.wait()


def interior(x0, w1, g, w2, sp, gp, step1=7, step2=4):
    proj = jax.ShapeDtypeStruct((C, E), BF)
    return pl.pallas_call(
        functools.partial(interior_kernel, step1, step2),
        name="interior_rows",
        out_shape=(jax.ShapeDtypeStruct((2, ROWS, COLS, 3 * C), BF),
                   jax.ShapeDtypeStruct((2, 14, COLS, 3 * C), BF),
                   jax.ShapeDtypeStruct((2, 12, COLS, C), F32),
                   jax.ShapeDtypeStruct((2, 8, C), F32), jax.ShapeDtypeStruct(x0.shape, BF),
                   jax.ShapeDtypeStruct(w2.shape, BF), proj, proj),
        in_specs=[VM] * 2 + [HBM] * 4,
        out_specs=(VM,) * 8,
        scratch_shapes=[pltpu.SemaphoreType.DMA((4,))],
        compiler_params=pltpu.CompilerParams(vmem_limit_bytes=24 * MIB),
        cost_estimate=pl.CostEstimate(flops=4_200_000_000, transcendentals=0, bytes_accessed=6_000_000),
    )(x0, w1, *in_hbm(g, w2, sp, gp))


def edge_kernel(label, sharp, cross, chip, x0, x1, xw, hw, sums, w1, w2, inner, o, copies, temp, out_hbm, halo, hh, sems):
    outs = [pltpu.make_async_copy(inner.at[f], out_hbm.at[f, 0, pl.ds(2, ROWS - 4)], sems.at[f]) for f in range(2)]
    for cp in outs:
        cp.start()
    temp[...] = jnp.full((8, 128), sharp[0], F32)
    here, strips = lax.axis_index("strip"), lax.axis_size("strip")
    odd = lax.rem(here, 2)
    for f in range(2):
        for r in range(2):
            halo[2 * f + 1 - odd, r] = widen(jnp.maximum(chip[f, r].astype(F32), 0.0))
            halo[2 * f + odd, r] = widen(jnp.maximum(cross[f, r].astype(F32), 0.0))
    for k in range(4):
        f = k // 2
        if k % 2 == 0:
            rows = [halo[k, 0], halo[k, 1], xw[f, 0], xw[f, 1]]
        else:
            rows = [xw[f, ROWS - 2], xw[f, ROWS - 1], halo[k, 0], halo[k, 1]]
        h = jnp.maximum(conv_of(rows, w1), 0.0)
        for r in range(2):
            row = h[r * COLS:(r + 1) * COLS]
            if k % 2 == 0 and r == 0:
                row = jnp.where(here > 0, row, 0.0)
            if k % 2 == 1 and r == 1:
                row = jnp.where(here < strips - 1, row, 0.0)
            hh[k, r] = widen(row)
    tot = [sums[0], sums[1]]
    for k in range(4):
        f = k // 2
        if k % 2 == 0:
            rows = [hh[k, 0], hh[k, 1], hw[f, 0], hw[f, 1]]
        else:
            rows = [hw[f, 12], hw[f, 13], hh[k, 0], hh[k, 1]]
        y = conv_of(rows, w2)
        y = jnp.maximum(y + (x0, x1)[f][0, 14 * (k % 2):14 * (k % 2) + 2].reshape(2 * COLS, C).astype(F32), 0.0)
        o[k] = y.reshape(2, COLS, C)
        tot[f] = tot[f] + jnp.sum(y.reshape(16, 8, C), axis=0)
    scale = 1.0 / (strips * ROWS * COLS)
    mark = jnp.full((1, 128), label[0], jnp.int32).astype(F32) * (1.0 / strips)
    for f in range(2):
        row = jnp.concatenate([jnp.sum(tot[f], axis=0, keepdims=True) * scale, mark], axis=1)
        for n in range(copies.shape[0]):
            copies[n, f:f + 1] = row
    for cp in outs:
        cp.wait()


def edges(label, sharp, cross, chip, x0, x1, xw, hw, sums, w1, w2, inner, members):
    return pl.pallas_call(
        edge_kernel,
        name="edge_rows",
        out_shape=(jax.ShapeDtypeStruct((4, 2, COLS, C), F32), jax.ShapeDtypeStruct((members, 2, C + 128), F32),
                   jax.ShapeDtypeStruct((8, 128), F32), jax.ShapeDtypeStruct((2, 1, ROWS, COLS, C), F32)),
        in_specs=[SM] * 2 + [VM] * 10,
        out_specs=(VM, VM, VM, HBM),
        scratch_shapes=[
            pltpu.VMEM((4, 2, COLS, 3 * C), BF),
            pltpu.VMEM((4, 2, COLS, 3 * C), BF),
            pltpu.SemaphoreType.DMA((2,)),
        ],
        compiler_params=pltpu.CompilerParams(vmem_limit_bytes=24 * MIB),
        cost_estimate=pl.CostEstimate(flops=1_200_000_000, transcendentals=0, bytes_accessed=4_000_000),
    )(label, sharp, cross, chip, x0, x1, xw, hw, sums, w1, w2, inner)


def head_kernel(sharp, tot, sproj, gproj, oe, partial_hbm, loss_ref, gs_hbm, gg_hbm, out_hbm, buf, sem, osem):
    outs = []
    for k in range(4):
        outs.append(pltpu.make_async_copy(oe.at[k], out_hbm.at[k // 2, 0, pl.ds((ROWS - 2) * (k % 2), 2)], osem.at[k]))
        outs[-1].start()
    pairs = tot.shape[1]
    s_pool = tot[0, :, :C].astype(BF)
    g_pool = tot[1, :, :C].astype(BF)
    label = tot[0, :, C:C + 1]
    temp = sharp[0:1, 0:1]
    s_emb = jnp.dot(s_pool, sproj[...], preferred_element_type=F32)
    g_emb = jnp.dot(g_pool, gproj[...], preferred_element_type=F32)
    s_inv = lax.rsqrt(jnp.sum(s_emb * s_emb, axis=-1, keepdims=True) + 1e-06)
    g_inv = lax.rsqrt(jnp.sum(g_emb * g_emb, axis=-1, keepdims=True) + 1e-06)
    s_unit = s_emb * s_inv
    g_unit = g_emb * g_inv
    s_bf = s_unit.astype(BF)
    g_bf = g_unit.astype(BF)
    logits = temp * lax.dot_general(s_bf, g_bf, (((1,), (1,)), ((), ())), preferred_element_type=F32)
    ex = jnp.exp(logits)
    row_total = jnp.sum(ex, axis=1, keepdims=True)
    column = lax.broadcasted_iota(jnp.int32, (pairs, pairs), 1).astype(F32)
    matched = column == label
    lgrad = (ex / row_total - jnp.where(matched, 1.0, 0.0)).astype(BF)

    def finish(k, unit_grad, unit, inverse, pool, dest):
        grad = ((unit_grad - unit * jnp.sum(unit * unit_grad, axis=-1, keepdims=True)) * inverse).astype(BF)
        for p in range(2):
            half = pl.ds(p * (C // 2), C // 2)
            buf[k, half] = lax.dot_general(pool[:, p * (C // 2):(p + 1) * (C // 2)], grad, (((0,), (0,)), ((), ())),
                                           preferred_element_type=F32)
            cp = pltpu.make_async_copy(buf.at[k, half], dest.at[half], sem.at[2 * k + p])
            cp.start()
            outs.append(cp)

    s_ug = temp * jnp.dot(lgrad, g_bf, preferred_element_type=F32)
    finish(0, s_ug, s_unit, s_inv, s_pool, gs_hbm)
    g_ug = temp * lax.dot_general(lgrad, s_bf, (((0,), (0,)), ((), ())), preferred_element_type=F32)
    finish(1, g_ug, g_unit, g_inv, g_pool, gg_hbm)
    positive = jnp.sum(jnp.where(matched, logits, 0.0), axis=1, keepdims=True)
    losses = jnp.log(row_total) - positive
    row = lax.broadcasted_iota(jnp.int32, (pairs, 1), 0)
    loss_ref[0] = jnp.sum(jnp.where(row == lax.axis_index("batch"), losses, 0.0))
    for cp in outs:
        cp.wait()


def head(sharp, tot, sproj, gproj, oe, out):
    return pl.pallas_call(
        head_kernel,
        name="contrastive_head",
        out_shape=(jax.ShapeDtypeStruct((1,), F32), jax.ShapeDtypeStruct((C, E), F32),
                   jax.ShapeDtypeStruct((C, E), F32), jax.ShapeDtypeStruct(out.shape, F32)),
        in_specs=[VM] * 5 + [HBM],
        out_specs=(SM, HBM, HBM, HBM),
        input_output_aliases={5: 3},
        scratch_shapes=[pltpu.VMEM((2, C, E), F32), pltpu.SemaphoreType.DMA((4,)), pltpu.SemaphoreType.DMA((4,))],
        compiler_params=pltpu.CompilerParams(vmem_limit_bytes=16 * MIB),
    )(sharp, tot, sproj, gproj, oe, out)


def gather_groups(batch, strips, inner):
    lines = {}
    for b in range(batch):
        for s in range(strips):
            half, plane = divmod(b, batch // 2)
            lines.setdefault(plane if inner else (half, s), []).append(b * strips + s)
    return list(lines.values())


def shards(state_maps, goal_maps, conv_one, conv_two, state_proj, goal_proj, inv_temp, pair_index):
    strips, batch = lax.axis_size("strip"), lax.axis_size("batch")
    w1 = conv_one.reshape(3, 3 * C, C)
    w2 = conv_two.reshape(3, 3 * C, C)
    cross, chip, x0, w1 = load(state_maps, goal_maps, w1)
    cross = lax.ppermute(cross, "strip", [(i, i + 2 * (i % 2) - 1) for i in range(1, strips - 1)])
    chip = lax.ppermute(chip, "strip", [(i, i ^ 1) for i in range(strips)])
    xw, hw, inner, sums, x1, w2, sp, gp = interior(x0, w1, goal_maps, w2, state_proj, goal_proj)
    oe, copies, temp, out = edges(
        pair_index, inv_temp, cross, chip, x0, x1, xw, hw, sums, w1, w2, inner, 2 * strips)
    both = ("batch", "strip")
    line = lax.all_to_all(copies, both, 0, 0, tiled=True, axis_index_groups=gather_groups(batch, strips, True))
    means = jnp.sum(line.reshape(2, strips, 2, C + 128), axis=1).astype(BF).reshape(4, C + 128)
    copies = jnp.broadcast_to(means, (batch // 2, 4, C + 128))
    got = lax.all_to_all(copies, both, 0, 0, tiled=True, axis_index_groups=gather_groups(batch, strips, False))
    tot = jnp.transpose(got.reshape(batch // 2, 2, 2, C + 128).astype(F32), (2, 1, 0, 3)).reshape(2, batch, C + 128)
    return head(temp, tot, sp, gp, oe, out)


def solution(mesh):
    placed = (
        P("batch", "strip", None, None),
        P("batch", "strip", None, None),
        P(),
        P(),
        P(),
        P(),
        P(),
        P("batch"),
    )
    return jax.shard_map(
        shards,
        mesh=mesh,
        in_specs=placed,
        out_specs=(P("batch"), P(), P(), P(None, "batch", "strip", None, None)),
        check_vma=False,
    )
```

```python
import functools
import jax
import jax.numpy as jnp
from jax import lax
from jax.experimental import pallas as pl
from jax.experimental.pallas import tpu as pltpu
from jax.sharding import PartitionSpec as P

ROWS, COLS, C, E = 16, 64, 256, 1024
BF, F32 = jnp.bfloat16, jnp.float32
MIB = 1 << 20
HBM = pl.BlockSpec(memory_space=pltpu.MemorySpace.HBM)
VM = pl.BlockSpec(memory_space=pltpu.MemorySpace.VMEM)
SM = pl.BlockSpec(memory_space=pltpu.MemorySpace.SMEM)


def in_hbm(*arrays):
    return [pltpu.with_memory_space_constraint(a, pltpu.MemorySpace.HBM) for a in arrays]


def load_kernel(s_hbm, g_hbm, w1_hbm, cross, chip, x, w1, sems):
    odd = lax.rem(lax.axis_index("strip"), 2)
    copies = []
    for f, ref in enumerate((s_hbm, g_hbm)):
        tail = (ROWS - 2) * (1 - odd)
        head = (ROWS - 2) * odd
        copies.append((ref.at[0, pl.ds(tail, 2)], chip.at[f]))
        copies.append((ref.at[0, pl.ds(head, 2)], cross.at[f]))
    copies.append((s_hbm.at[0], x.at[0]))
    for dy in range(3):
        copies.append((w1_hbm.at[dy], w1.at[dy]))
    copies = [pltpu.make_async_copy(a, b, sems.at[k]) for k, (a, b) in enumerate(copies)]
    for cp in copies:
        cp.start()
    for cp in copies:
        cp.wait()


def load(s, g, w1):
    side = jax.ShapeDtypeStruct((2, 2, COLS, C), BF)
    return pl.pallas_call(
        load_kernel,
        name="load_rows",
        out_shape=(side, side, jax.ShapeDtypeStruct((1, ROWS, COLS, C), BF), jax.ShapeDtypeStruct(w1.shape, BF)),
        in_specs=[HBM] * 3,
        out_specs=(VM,) * 4,
        scratch_shapes=[pltpu.SemaphoreType.DMA((8,))],
        compiler_params=pltpu.CompilerParams(vmem_limit_bytes=8 * MIB),
    )(*in_hbm(s, g, w1))


def widen(row):
    col = lax.broadcasted_iota(jnp.int32, row.shape, 0)
    left = jnp.where(col == 0, 0.0, pltpu.roll(row, 1, 0))
    right = jnp.where(col == COLS - 1, 0.0, pltpu.roll(row, COLS - 1, 0))
    return jnp.concatenate([left.astype(BF), row.astype(BF), right.astype(BF)], axis=-1)


def conv(wide, first, rows, weights):
    total = None
    for dy in range(3):
        lhs = wide[pl.ds(first + dy, rows)].reshape(rows * COLS, 3 * C)
        part = jnp.dot(lhs, weights[dy], preferred_element_type=F32)
        total = part if total is None else total + part
    return total


def conv_of(rows, weights):
    total = None
    for dy in range(3):
        lhs = jnp.concatenate([rows[dy], rows[dy + 1]], axis=0)
        part = jnp.dot(lhs, weights[dy], preferred_element_type=F32)
        total = part if total is None else total + part
    return total


def spans(total, step):
    return [(r, min(step, total - r)) for r in range(0, total, step)]


def interior_kernel(step1, step2, x0, w1, g_hbm, w2_hbm, sp_hbm, gp_hbm, xw, hw, o, sum_ref, x1, w2, sp, gp, out_hbm, sems):
    cw2 = pltpu.make_async_copy(w2_hbm, w2, sems.at[0])
    csp = pltpu.make_async_copy(sp_hbm, sp, sems.at[1])
    cgp = pltpu.make_async_copy(gp_hbm, gp, sems.at[2])
    cx1 = pltpu.make_async_copy(g_hbm.at[0], x1.at[0], sems.at[3])
    cw2.start(); cx1.start(); csp.start(); cgp.start()
    x = (x0.at[0], x1.at[0])

    def spread(f, rows):
        for r in rows:
            xw[f, r] = widen(jnp.maximum(x[f][r].astype(F32), 0.0))

    def first(f, r, n):
        h = jnp.maximum(conv(xw.at[f], r, n, w1), 0.0)
        for k in range(n):
            hw[f, r + k] = widen(h[k * COLS:(k + 1) * COLS])

    def second(f, r, n, acc):
        y = conv(hw.at[f], r, n, w2)
        y = jnp.maximum(y + x[f][r + 2:r + 2 + n].reshape(n * COLS, C).astype(F32), 0.0)
        o[f, r:r + n] = y.reshape(n, COLS, C)
        part = jnp.sum(y.reshape(n * COLS // 8, 8, C), axis=0)
        return part if acc is None else acc + part

    spread(0, range(step1 + 2))
    plan = spans(14, step1)
    done = step1 + 2
    for i, (r, n) in enumerate(plan):
        if i + 1 < len(plan):
            upto = plan[i + 1][0] + plan[i + 1][1] + 2
            spread(0, range(done, upto))
            done = upto
        first(0, r, n)
    cw2.wait(); cx1.wait()
    acc = None
    plan = spans(12, step2)
    for i, (r, n) in enumerate(plan):
        spread(1, range(i * 16 // len(plan), (i + 1) * 16 // len(plan)))
        acc = second(0, r, n, acc)
    sum_ref[0] = acc
    cout = pltpu.make_async_copy(o.at[0], out_hbm.at[0, 0, pl.ds(2, ROWS - 4)], sems.at[4])
    cout.start()
    for r, n in spans(14, step1):
        first(1, r, n)
    acc = None
    for r, n in spans(12, step2):
        acc = second(1, r, n, acc)
    sum_ref[1] = acc
    csp.wait(); cgp.wait(); cout.wait()


def interior(x0, w1, g, w2, sp, gp, step1=7, step2=4):
    proj = jax.ShapeDtypeStruct((C, E), BF)
    return pl.pallas_call(
        functools.partial(interior_kernel, step1, step2),
        name="interior_rows",
        out_shape=(jax.ShapeDtypeStruct((2, ROWS, COLS, 3 * C), BF),
                   jax.ShapeDtypeStruct((2, 14, COLS, 3 * C), BF),
                   jax.ShapeDtypeStruct((2, 12, COLS, C), F32),
                   jax.ShapeDtypeStruct((2, 8, C), F32), jax.ShapeDtypeStruct(x0.shape, BF),
                   jax.ShapeDtypeStruct(w2.shape, BF), proj, proj,
                   jax.ShapeDtypeStruct((2, 1, ROWS, COLS, C), F32)),
        in_specs=[VM] * 2 + [HBM] * 4,
        out_specs=(VM,) * 8 + (HBM,),
        scratch_shapes=[pltpu.SemaphoreType.DMA((5,))],
        compiler_params=pltpu.CompilerParams(vmem_limit_bytes=24 * MIB),
        cost_estimate=pl.CostEstimate(flops=4_200_000_000, transcendentals=0, bytes_accessed=6_000_000),
    )(x0, w1, *in_hbm(g, w2, sp, gp))


def edge_kernel(label, sharp, cross, chip, x0, x1, xw, hw, sums, w1, w2, inner, partial_hbm,
                o, copies, temp, out_hbm, halo, hh, sem):
    cout = pltpu.make_async_copy(inner.at[1], out_hbm.at[1, 0, pl.ds(2, ROWS - 4)], sem)
    cout.start()
    temp[...] = jnp.full((8, 128), sharp[0], F32)
    here, strips = lax.axis_index("strip"), lax.axis_size("strip")
    odd = lax.rem(here, 2)
    for f in range(2):
        for r in range(2):
            halo[2 * f + 1 - odd, r] = widen(jnp.maximum(chip[f, r].astype(F32), 0.0))
            halo[2 * f + odd, r] = widen(jnp.maximum(cross[f, r].astype(F32), 0.0))
    for k in range(4):
        f = k // 2
        if k % 2 == 0:
            rows = [halo[k, 0], halo[k, 1], xw[f, 0], xw[f, 1]]
        else:
            rows = [xw[f, ROWS - 2], xw[f, ROWS - 1], halo[k, 0], halo[k, 1]]
        h = jnp.maximum(conv_of(rows, w1), 0.0)
        for r in range(2):
            row = h[r * COLS:(r + 1) * COLS]
            if k % 2 == 0 and r == 0:
                row = jnp.where(here > 0, row, 0.0)
            if k % 2 == 1 and r == 1:
                row = jnp.where(here < strips - 1, row, 0.0)
            hh[k, r] = widen(row)
    tot = [sums[0], sums[1]]
    for k in range(4):
        f = k // 2
        if k % 2 == 0:
            rows = [hh[k, 0], hh[k, 1], hw[f, 0], hw[f, 1]]
        else:
            rows = [hw[f, 12], hw[f, 13], hh[k, 0], hh[k, 1]]
        y = conv_of(rows, w2)
        y = jnp.maximum(y + (x0, x1)[f][0, 14 * (k % 2):14 * (k % 2) + 2].reshape(2 * COLS, C).astype(F32), 0.0)
        o[k] = y.reshape(2, COLS, C)
        tot[f] = tot[f] + jnp.sum(y.reshape(16, 8, C), axis=0)
    scale = 1.0 / (strips * ROWS * COLS)
    mark = jnp.full((1, 128), label[0], jnp.int32).astype(F32) * (1.0 / strips)
    for f in range(2):
        row = jnp.concatenate([jnp.sum(tot[f], axis=0, keepdims=True) * scale, mark], axis=1)
        for n in range(copies.shape[0]):
            copies[n, f:f + 1] = row
    cout.wait()


def edges(label, sharp, cross, chip, x0, x1, xw, hw, sums, w1, w2, inner, out, members):
    return pl.pallas_call(
        edge_kernel,
        name="edge_rows",
        out_shape=(jax.ShapeDtypeStruct((4, 2, COLS, C), F32), jax.ShapeDtypeStruct((members, 2, C + 128), F32),
                   jax.ShapeDtypeStruct((8, 128), F32), jax.ShapeDtypeStruct(out.shape, F32)),
        in_specs=[SM] * 2 + [VM] * 10 + [HBM],
        out_specs=(VM, VM, VM, HBM),
        input_output_aliases={12: 3},
        scratch_shapes=[
            pltpu.VMEM((4, 2, COLS, 3 * C), BF),
            pltpu.VMEM((4, 2, COLS, 3 * C), BF),
            pltpu.SemaphoreType.DMA,
        ],
        compiler_params=pltpu.CompilerParams(vmem_limit_bytes=24 * MIB),
        cost_estimate=pl.CostEstimate(flops=1_200_000_000, transcendentals=0, bytes_accessed=4_000_000),
    )(label, sharp, cross, chip, x0, x1, xw, hw, sums, w1, w2, inner, out)


def head_kernel(sharp, tot, sproj, gproj, oe, partial_hbm, loss_ref, gs_hbm, gg_hbm, out_hbm, buf, sem, osem):
    outs = []
    for k in range(4):
        outs.append(pltpu.make_async_copy(oe.at[k], out_hbm.at[k // 2, 0, pl.ds((ROWS - 2) * (k % 2), 2)], osem.at[k]))
        outs[-1].start()
    pairs = tot.shape[1]
    s_pool = tot[0, :, :C].astype(BF)
    g_pool = tot[1, :, :C].astype(BF)
    label = tot[0, :, C:C + 1]
    temp = sharp[0:1, 0:1]
    s_emb = jnp.dot(s_pool, sproj[...], preferred_element_type=F32)
    g_emb = jnp.dot(g_pool, gproj[...], preferred_element_type=F32)
    s_inv = lax.rsqrt(jnp.sum(s_emb * s_emb, axis=-1, keepdims=True) + 1e-06)
    g_inv = lax.rsqrt(jnp.sum(g_emb * g_emb, axis=-1, keepdims=True) + 1e-06)
    s_unit = s_emb * s_inv
    g_unit = g_emb * g_inv
    s_bf = s_unit.astype(BF)
    g_bf = g_unit.astype(BF)
    logits = temp * lax.dot_general(s_bf, g_bf, (((1,), (1,)), ((), ())), preferred_element_type=F32)
    ex = jnp.exp(logits)
    row_total = jnp.sum(ex, axis=1, keepdims=True)
    column = lax.broadcasted_iota(jnp.int32, (pairs, pairs), 1).astype(F32)
    matched = column == label
    lgrad = (ex / row_total - jnp.where(matched, 1.0, 0.0)).astype(BF)

    def finish(k, unit_grad, unit, inverse, pool, dest):
        grad = ((unit_grad - unit * jnp.sum(unit * unit_grad, axis=-1, keepdims=True)) * inverse).astype(BF)
        for p in range(2):
            half = pl.ds(p * (C // 2), C // 2)
            buf[k, half] = lax.dot_general(pool[:, p * (C // 2):(p + 1) * (C // 2)], grad, (((0,), (0,)), ((), ())),
                                           preferred_element_type=F32)
            cp = pltpu.make_async_copy(buf.at[k, half], dest.at[half], sem.at[2 * k + p])
            cp.start()
            outs.append(cp)

    s_ug = temp * jnp.dot(lgrad, g_bf, preferred_element_type=F32)
    finish(0, s_ug, s_unit, s_inv, s_pool, gs_hbm)
    g_ug = temp * lax.dot_general(lgrad, s_bf, (((0,), (0,)), ((), ())), preferred_element_type=F32)
    finish(1, g_ug, g_unit, g_inv, g_pool, gg_hbm)
    positive = jnp.sum(jnp.where(matched, logits, 0.0), axis=1, keepdims=True)
    losses = jnp.log(row_total) - positive
    row = lax.broadcasted_iota(jnp.int32, (pairs, 1), 0)
    loss_ref[0] = jnp.sum(jnp.where(row == lax.axis_index("batch"), losses, 0.0))
    for cp in outs:
        cp.wait()


def head(sharp, tot, sproj, gproj, oe, out):
    return pl.pallas_call(
        head_kernel,
        name="contrastive_head",
        out_shape=(jax.ShapeDtypeStruct((1,), F32), jax.ShapeDtypeStruct((C, E), F32),
                   jax.ShapeDtypeStruct((C, E), F32), jax.ShapeDtypeStruct(out.shape, F32)),
        in_specs=[VM] * 5 + [HBM],
        out_specs=(SM, HBM, HBM, HBM),
        input_output_aliases={5: 3},
        scratch_shapes=[pltpu.VMEM((2, C, E), F32), pltpu.SemaphoreType.DMA((4,)), pltpu.SemaphoreType.DMA((4,))],
        compiler_params=pltpu.CompilerParams(vmem_limit_bytes=16 * MIB),
    )(sharp, tot, sproj, gproj, oe, out)


def gather_groups(batch, strips, inner):
    lines = {}
    for b in range(batch):
        for s in range(strips):
            half, plane = divmod(b, batch // 2)
            lines.setdefault(plane if inner else (half, s), []).append(b * strips + s)
    return list(lines.values())


def shards(state_maps, goal_maps, conv_one, conv_two, state_proj, goal_proj, inv_temp, pair_index):
    strips, batch = lax.axis_size("strip"), lax.axis_size("batch")
    w1 = conv_one.reshape(3, 3 * C, C)
    w2 = conv_two.reshape(3, 3 * C, C)
    cross, chip, x0, w1 = load(state_maps, goal_maps, w1)
    cross = lax.ppermute(cross, "strip", [(i, i + 2 * (i % 2) - 1) for i in range(1, strips - 1)])
    chip = lax.ppermute(chip, "strip", [(i, i ^ 1) for i in range(strips)])
    xw, hw, inner, sums, x1, w2, sp, gp, out = interior(x0, w1, goal_maps, w2, state_proj, goal_proj)
    oe, copies, temp, out = edges(
        pair_index, inv_temp, cross, chip, x0, x1, xw, hw, sums, w1, w2, inner, out, 2 * strips)
    both = ("batch", "strip")
    line = lax.all_to_all(copies, both, 0, 0, tiled=True, axis_index_groups=gather_groups(batch, strips, True))
    means = jnp.sum(line.reshape(2, strips, 2, C + 128), axis=1).astype(BF).reshape(4, C + 128)
    copies = jnp.broadcast_to(means, (batch // 2, 4, C + 128))
    got = lax.all_to_all(copies, both, 0, 0, tiled=True, axis_index_groups=gather_groups(batch, strips, False))
    tot = jnp.transpose(got.reshape(batch // 2, 2, 2, C + 128).astype(F32), (2, 1, 0, 3)).reshape(2, batch, C + 128)
    return head(temp, tot, sp, gp, oe, out)


def solution(mesh):
    placed = (
        P("batch", "strip", None, None),
        P("batch", "strip", None, None),
        P(),
        P(),
        P(),
        P(),
        P(),
        P("batch"),
    )
    return jax.shard_map(
        shards,
        mesh=mesh,
        in_specs=placed,
        out_specs=(P("batch"), P(), P(), P(None, "batch", "strip", None, None)),
        check_vma=False,
    )
```

```python
import functools
import jax
import jax.numpy as jnp
from jax import lax
from jax.experimental import pallas as pl
from jax.experimental.pallas import tpu as pltpu
from jax.sharding import PartitionSpec as P

ROWS, COLS, C, E = 16, 64, 256, 1024
BF, F32 = jnp.bfloat16, jnp.float32
MIB = 1 << 20
HBM = pl.BlockSpec(memory_space=pltpu.MemorySpace.HBM)
VM = pl.BlockSpec(memory_space=pltpu.MemorySpace.VMEM)
SM = pl.BlockSpec(memory_space=pltpu.MemorySpace.SMEM)


def in_hbm(*arrays):
    return [pltpu.with_memory_space_constraint(a, pltpu.MemorySpace.HBM) for a in arrays]


def load_kernel(s_hbm, g_hbm, w1_hbm, cross, chip, x, w1, sems):
    odd = lax.rem(lax.axis_index("strip"), 2)
    copies = []
    for f, ref in enumerate((s_hbm, g_hbm)):
        tail = (ROWS - 2) * (1 - odd)
        head = (ROWS - 2) * odd
        copies.append((ref.at[0, pl.ds(tail, 2)], chip.at[f]))
        copies.append((ref.at[0, pl.ds(head, 2)], cross.at[f]))
    copies.append((s_hbm.at[0], x.at[0]))
    for dy in range(3):
        copies.append((w1_hbm.at[dy], w1.at[dy]))
    copies = [pltpu.make_async_copy(a, b, sems.at[k]) for k, (a, b) in enumerate(copies)]
    for cp in copies:
        cp.start()
    for cp in copies:
        cp.wait()


def load(s, g, w1):
    side = jax.ShapeDtypeStruct((2, 2, COLS, C), BF)
    return pl.pallas_call(
        load_kernel,
        name="load_rows",
        out_shape=(side, side, jax.ShapeDtypeStruct((1, ROWS, COLS, C), BF), jax.ShapeDtypeStruct(w1.shape, BF)),
        in_specs=[HBM] * 3,
        out_specs=(VM,) * 4,
        scratch_shapes=[pltpu.SemaphoreType.DMA((8,))],
        compiler_params=pltpu.CompilerParams(vmem_limit_bytes=8 * MIB),
    )(*in_hbm(s, g, w1))


def widen(row):
    col = lax.broadcasted_iota(jnp.int32, row.shape, 0)
    left = jnp.where(col == 0, 0.0, pltpu.roll(row, 1, 0))
    right = jnp.where(col == COLS - 1, 0.0, pltpu.roll(row, COLS - 1, 0))
    return jnp.concatenate([left.astype(BF), row.astype(BF), right.astype(BF)], axis=-1)


def conv(wide, first, rows, weights):
    total = None
    for dy in range(3):
        lhs = wide[pl.ds(first + dy, rows)].reshape(rows * COLS, 3 * C)
        part = jnp.dot(lhs, weights[dy], preferred_element_type=F32)
        total = part if total is None else total + part
    return total


def conv_of(rows, weights):
    total = None
    for dy in range(3):
        lhs = jnp.concatenate([rows[dy], rows[dy + 1]], axis=0)
        part = jnp.dot(lhs, weights[dy], preferred_element_type=F32)
        total = part if total is None else total + part
    return total


def spans(total, step):
    return [(r, min(step, total - r)) for r in range(0, total, step)]


def interior_kernel(step1, step2, x0, w1, g_hbm, w2_hbm, sp_hbm, gp_hbm, xw, hw, o, sum_ref, x1, w2, sp, gp, out_hbm, sems):
    cw2 = pltpu.make_async_copy(w2_hbm, w2, sems.at[0])
    csp = pltpu.make_async_copy(sp_hbm, sp, sems.at[1])
    cgp = pltpu.make_async_copy(gp_hbm, gp, sems.at[2])
    cx1 = pltpu.make_async_copy(g_hbm.at[0], x1.at[0], sems.at[3])
    cw2.start(); cx1.start(); csp.start(); cgp.start()
    x = (x0.at[0], x1.at[0])

    def spread(f, rows):
        for r in rows:
            xw[f, r] = widen(jnp.maximum(x[f][r].astype(F32), 0.0))

    def first(f, r, n):
        h = jnp.maximum(conv(xw.at[f], r, n, w1), 0.0)
        for k in range(n):
            hw[f, r + k] = widen(h[k * COLS:(k + 1) * COLS])

    def second(f, r, n, acc):
        y = conv(hw.at[f], r, n, w2)
        y = jnp.maximum(y + x[f][r + 2:r + 2 + n].reshape(n * COLS, C).astype(F32), 0.0)
        o[f, r:r + n] = y.reshape(n, COLS, C)
        part = jnp.sum(y.reshape(n * COLS // 8, 8, C), axis=0)
        return part if acc is None else acc + part

    spread(0, range(step1 + 2))
    plan = spans(14, step1)
    done = step1 + 2
    for i, (r, n) in enumerate(plan):
        if i + 1 < len(plan):
            upto = plan[i + 1][0] + plan[i + 1][1] + 2
            spread(0, range(done, upto))
            done = upto
        first(0, r, n)
    cw2.wait(); cx1.wait()
    acc = None
    plan = spans(12, step2)
    for i, (r, n) in enumerate(plan):
        spread(1, range(i * 16 // len(plan), (i + 1) * 16 // len(plan)))
        acc = second(0, r, n, acc)
    sum_ref[0] = acc
    cout = pltpu.make_async_copy(o.at[0], out_hbm.at[0, 0, pl.ds(2, ROWS - 4)], sems.at[4])
    cout.start()
    for r, n in spans(14, step1):
        first(1, r, n)
    acc = None
    for r, n in spans(12, step2):
        acc = second(1, r, n, acc)
    sum_ref[1] = acc
    csp.wait(); cgp.wait(); cout.wait()


def interior(x0, w1, g, w2, sp, gp, step1=7, step2=4):
    proj = jax.ShapeDtypeStruct((C, E), BF)
    return pl.pallas_call(
        functools.partial(interior_kernel, step1, step2),
        name="interior_rows",
        out_shape=(jax.ShapeDtypeStruct((2, ROWS, COLS, 3 * C), BF),
                   jax.ShapeDtypeStruct((2, 14, COLS, 3 * C), BF),
                   jax.ShapeDtypeStruct((2, 12, COLS, C), F32),
                   jax.ShapeDtypeStruct((2, 8, C), F32), jax.ShapeDtypeStruct(x0.shape, BF),
                   jax.ShapeDtypeStruct(w2.shape, BF), proj, proj,
                   jax.ShapeDtypeStruct((2, 1, ROWS, COLS, C), F32)),
        in_specs=[VM] * 2 + [HBM] * 4,
        out_specs=(VM,) * 8 + (HBM,),
        scratch_shapes=[pltpu.SemaphoreType.DMA((5,))],
        compiler_params=pltpu.CompilerParams(vmem_limit_bytes=24 * MIB),
        cost_estimate=pl.CostEstimate(flops=4_200_000_000, transcendentals=0, bytes_accessed=6_000_000),
    )(x0, w1, *in_hbm(g, w2, sp, gp))


def edge_kernel(label, sharp, chip, cross, x0, x1, xw, hw, sums, w1, w2, inner, partial_hbm,
                o, copies, temp, out_hbm, halo, hh, sem):
    cout = pltpu.make_async_copy(inner.at[1], out_hbm.at[1, 0, pl.ds(2, ROWS - 4)], sem)
    cout.start()
    temp[...] = jnp.full((8, 128), sharp[0], F32)
    here, strips = lax.axis_index("strip"), lax.axis_size("strip")
    odd = lax.rem(here, 2)
    for f in range(2):
        for r in range(2):
            halo[2 * f + 1 - odd, r] = widen(jnp.maximum(chip[f, r].astype(F32), 0.0))
            halo[2 * f + odd, r] = widen(jnp.maximum(cross[f, r].astype(F32), 0.0))
    for k in range(4):
        f = k // 2
        if k % 2 == 0:
            rows = [halo[k, 0], halo[k, 1], xw[f, 0], xw[f, 1]]
        else:
            rows = [xw[f, ROWS - 2], xw[f, ROWS - 1], halo[k, 0], halo[k, 1]]
        h = jnp.maximum(conv_of(rows, w1), 0.0)
        for r in range(2):
            row = h[r * COLS:(r + 1) * COLS]
            if k % 2 == 0 and r == 0:
                row = jnp.where(here > 0, row, 0.0)
            if k % 2 == 1 and r == 1:
                row = jnp.where(here < strips - 1, row, 0.0)
            hh[k, r] = widen(row)
    tot = [sums[0], sums[1]]
    for k in range(4):
        f = k // 2
        if k % 2 == 0:
            rows = [hh[k, 0], hh[k, 1], hw[f, 0], hw[f, 1]]
        else:
            rows = [hw[f, 12], hw[f, 13], hh[k, 0], hh[k, 1]]
        y = conv_of(rows, w2)
        y = jnp.maximum(y + (x0, x1)[f][0, 14 * (k % 2):14 * (k % 2) + 2].reshape(2 * COLS, C).astype(F32), 0.0)
        o[k] = y.reshape(2, COLS, C)
        tot[f] = tot[f] + jnp.sum(y.reshape(16, 8, C), axis=0)
    scale = 1.0 / (strips * ROWS * COLS)
    mark = jnp.full((1, 128), label[0], jnp.int32).astype(F32) * (1.0 / strips)
    for f in range(2):
        row = jnp.concatenate([jnp.sum(tot[f], axis=0, keepdims=True) * scale, mark], axis=1)
        for n in range(copies.shape[0]):
            copies[n, f:f + 1] = row
    cout.wait()


def edges(label, sharp, cross, chip, x0, x1, xw, hw, sums, w1, w2, inner, out, members):
    return pl.pallas_call(
        edge_kernel,
        name="edge_rows",
        out_shape=(jax.ShapeDtypeStruct((4, 2, COLS, C), F32), jax.ShapeDtypeStruct((members, 2, C + 128), F32),
                   jax.ShapeDtypeStruct((8, 128), F32), jax.ShapeDtypeStruct(out.shape, F32)),
        in_specs=[SM] * 2 + [VM] * 10 + [HBM],
        out_specs=(VM, VM, VM, HBM),
        input_output_aliases={12: 3},
        scratch_shapes=[
            pltpu.VMEM((4, 2, COLS, 3 * C), BF),
            pltpu.VMEM((4, 2, COLS, 3 * C), BF),
            pltpu.SemaphoreType.DMA,
        ],
        compiler_params=pltpu.CompilerParams(vmem_limit_bytes=24 * MIB),
        cost_estimate=pl.CostEstimate(flops=1_200_000_000, transcendentals=0, bytes_accessed=4_000_000),
    )(label, sharp, chip, cross, x0, x1, xw, hw, sums, w1, w2, inner, out)


def head_kernel(sharp, tot, sproj, gproj, oe, partial_hbm, loss_ref, gs_hbm, gg_hbm, out_hbm, buf, sem, osem):
    outs = []
    for k in range(4):
        outs.append(pltpu.make_async_copy(oe.at[k], out_hbm.at[k // 2, 0, pl.ds((ROWS - 2) * (k % 2), 2)], osem.at[k]))
        outs[-1].start()
    pairs = tot.shape[1]
    s_pool = tot[0, :, :C].astype(BF)
    g_pool = tot[1, :, :C].astype(BF)
    label = tot[0, :, C:C + 1]
    temp = sharp[0:1, 0:1]
    s_emb = jnp.dot(s_pool, sproj[...], preferred_element_type=F32)
    g_emb = jnp.dot(g_pool, gproj[...], preferred_element_type=F32)
    s_inv = lax.rsqrt(jnp.sum(s_emb * s_emb, axis=-1, keepdims=True) + 1e-06)
    g_inv = lax.rsqrt(jnp.sum(g_emb * g_emb, axis=-1, keepdims=True) + 1e-06)
    s_unit = s_emb * s_inv
    g_unit = g_emb * g_inv
    s_bf = s_unit.astype(BF)
    g_bf = g_unit.astype(BF)
    logits = temp * lax.dot_general(s_bf, g_bf, (((1,), (1,)), ((), ())), preferred_element_type=F32)
    ex = jnp.exp(logits)
    row_total = jnp.sum(ex, axis=1, keepdims=True)
    column = lax.broadcasted_iota(jnp.int32, (pairs, pairs), 1).astype(F32)
    matched = column == label
    lgrad = (ex / row_total - jnp.where(matched, 1.0, 0.0)).astype(BF)

    def finish(k, unit_grad, unit, inverse, pool, dest):
        grad = ((unit_grad - unit * jnp.sum(unit * unit_grad, axis=-1, keepdims=True)) * inverse).astype(BF)
        for p in range(2):
            half = pl.ds(p * (C // 2), C // 2)
            buf[k, half] = lax.dot_general(pool[:, p * (C // 2):(p + 1) * (C // 2)], grad, (((0,), (0,)), ((), ())),
                                           preferred_element_type=F32)
            cp = pltpu.make_async_copy(buf.at[k, half], dest.at[half], sem.at[2 * k + p])
            cp.start()
            outs.append(cp)

    s_ug = temp * jnp.dot(lgrad, g_bf, preferred_element_type=F32)
    finish(0, s_ug, s_unit, s_inv, s_pool, gs_hbm)
    g_ug = temp * lax.dot_general(lgrad, s_bf, (((0,), (0,)), ((), ())), preferred_element_type=F32)
    finish(1, g_ug, g_unit, g_inv, g_pool, gg_hbm)
    positive = jnp.sum(jnp.where(matched, logits, 0.0), axis=1, keepdims=True)
    losses = jnp.log(row_total) - positive
    row = lax.broadcasted_iota(jnp.int32, (pairs, 1), 0)
    loss_ref[0] = jnp.sum(jnp.where(row == lax.axis_index("batch"), losses, 0.0))
    for cp in outs:
        cp.wait()


def head(sharp, tot, sproj, gproj, oe, out):
    return pl.pallas_call(
        head_kernel,
        name="contrastive_head",
        out_shape=(jax.ShapeDtypeStruct((1,), F32), jax.ShapeDtypeStruct((C, E), F32),
                   jax.ShapeDtypeStruct((C, E), F32), jax.ShapeDtypeStruct(out.shape, F32)),
        in_specs=[VM] * 5 + [HBM],
        out_specs=(SM, HBM, HBM, HBM),
        input_output_aliases={5: 3},
        scratch_shapes=[pltpu.VMEM((2, C, E), F32), pltpu.SemaphoreType.DMA((4,)), pltpu.SemaphoreType.DMA((4,))],
        compiler_params=pltpu.CompilerParams(vmem_limit_bytes=16 * MIB),
    )(sharp, tot, sproj, gproj, oe, out)


def gather_groups(batch, strips, inner):
    lines = {}
    for b in range(batch):
        for s in range(strips):
            half, plane = divmod(b, batch // 2)
            lines.setdefault(plane if inner else (half, s), []).append(b * strips + s)
    return list(lines.values())


def shards(state_maps, goal_maps, conv_one, conv_two, state_proj, goal_proj, inv_temp, pair_index):
    strips, batch = lax.axis_size("strip"), lax.axis_size("batch")
    w1 = conv_one.reshape(3, 3 * C, C)
    w2 = conv_two.reshape(3, 3 * C, C)
    cross, chip, x0, w1 = load(state_maps, goal_maps, w1)
    cross = lax.ppermute(cross, "strip", [(i, i + 2 * (i % 2) - 1) for i in range(1, strips - 1)])
    chip = lax.ppermute(chip, "strip", [(i, i ^ 1) for i in range(strips)])
    xw, hw, inner, sums, x1, w2, sp, gp, out = interior(x0, w1, goal_maps, w2, state_proj, goal_proj)
    oe, copies, temp, out = edges(
        pair_index, inv_temp, cross, chip, x0, x1, xw, hw, sums, w1, w2, inner, out, 2 * strips)
    both = ("batch", "strip")
    line = lax.all_to_all(copies, both, 0, 0, tiled=True, axis_index_groups=gather_groups(batch, strips, True))
    means = jnp.sum(line.reshape(2, strips, 2, C + 128), axis=1).astype(BF).reshape(4, C + 128)
    copies = jnp.broadcast_to(means, (batch // 2, 4, C + 128))
    got = lax.all_to_all(copies, both, 0, 0, tiled=True, axis_index_groups=gather_groups(batch, strips, False))
    tot = jnp.transpose(got.reshape(batch // 2, 2, 2, C + 128).astype(F32), (2, 1, 0, 3)).reshape(2, batch, C + 128)
    return head(temp, tot, sp, gp, oe, out)


def solution(mesh):
    placed = (
        P("batch", "strip", None, None),
        P("batch", "strip", None, None),
        P(),
        P(),
        P(),
        P(),
        P(),
        P("batch"),
    )
    return jax.shard_map(
        shards,
        mesh=mesh,
        in_specs=placed,
        out_specs=(P("batch"), P(), P(), P(None, "batch", "strip", None, None)),
        check_vma=False,
    )
```

```python
import functools
import jax
import jax.numpy as jnp
from jax import lax
from jax.experimental import pallas as pl
from jax.experimental.pallas import tpu as pltpu
from jax.sharding import PartitionSpec as P

ROWS, COLS, C, E = 16, 64, 256, 1024
BF, F32 = jnp.bfloat16, jnp.float32
MIB = 1 << 20
HBM = pl.BlockSpec(memory_space=pltpu.MemorySpace.HBM)
VM = pl.BlockSpec(memory_space=pltpu.MemorySpace.VMEM)
SM = pl.BlockSpec(memory_space=pltpu.MemorySpace.SMEM)


def in_hbm(*arrays):
    return [pltpu.with_memory_space_constraint(a, pltpu.MemorySpace.HBM) for a in arrays]


def load_kernel(s_hbm, g_hbm, w1_hbm, cross, chip, x, w1, sems):
    odd = lax.rem(lax.axis_index("strip"), 2)
    copies = []
    for f, ref in enumerate((s_hbm, g_hbm)):
        tail = (ROWS - 2) * (1 - odd)
        head = (ROWS - 2) * odd
        copies.append((ref.at[0, pl.ds(tail, 2)], chip.at[f]))
        copies.append((ref.at[0, pl.ds(head, 2)], cross.at[f]))
    copies.append((s_hbm.at[0], x.at[0]))
    for dy in range(3):
        copies.append((w1_hbm.at[dy], w1.at[dy]))
    copies = [pltpu.make_async_copy(a, b, sems.at[k]) for k, (a, b) in enumerate(copies)]
    for cp in copies:
        cp.start()
    for cp in copies:
        cp.wait()


def load(s, g, w1):
    side = jax.ShapeDtypeStruct((2, 2, COLS, C), BF)
    return pl.pallas_call(
        load_kernel,
        name="load_rows",
        out_shape=(side, side, jax.ShapeDtypeStruct((1, ROWS, COLS, C), BF), jax.ShapeDtypeStruct(w1.shape, BF)),
        in_specs=[HBM] * 3,
        out_specs=(VM,) * 4,
        scratch_shapes=[pltpu.SemaphoreType.DMA((8,))],
        compiler_params=pltpu.CompilerParams(vmem_limit_bytes=8 * MIB),
    )(*in_hbm(s, g, w1))


def widen(row):
    col = lax.broadcasted_iota(jnp.int32, row.shape, 0)
    left = jnp.where(col == 0, 0.0, pltpu.roll(row, 1, 0))
    right = jnp.where(col == COLS - 1, 0.0, pltpu.roll(row, COLS - 1, 0))
    return jnp.concatenate([left.astype(BF), row.astype(BF), right.astype(BF)], axis=-1)


def conv(wide, first, rows, weights):
    total = None
    for dy in range(3):
        lhs = wide[pl.ds(first + dy, rows)].reshape(rows * COLS, 3 * C)
        part = jnp.dot(lhs, weights[dy], preferred_element_type=F32)
        total = part if total is None else total + part
    return total


def conv_of(rows, weights):
    total = None
    for dy in range(3):
        lhs = jnp.concatenate([rows[dy], rows[dy + 1]], axis=0)
        part = jnp.dot(lhs, weights[dy], preferred_element_type=F32)
        total = part if total is None else total + part
    return total


def spans(total, step):
    return [(r, min(step, total - r)) for r in range(0, total, step)]


def interior_kernel(step1, step2, x0, w1, g_hbm, w2_hbm, sp_hbm, gp_hbm, xw, hw, o, sum_ref, x1, w2, sp, gp, out_hbm, sems):
    cw2 = pltpu.make_async_copy(w2_hbm, w2, sems.at[0])
    csp = pltpu.make_async_copy(sp_hbm, sp, sems.at[1])
    cgp = pltpu.make_async_copy(gp_hbm, gp, sems.at[2])
    cx1 = pltpu.make_async_copy(g_hbm.at[0], x1.at[0], sems.at[3])
    cw2.start(); cx1.start(); csp.start(); cgp.start()
    x = (x0.at[0], x1.at[0])

    def spread(f, rows):
        for r in rows:
            xw[f, r] = widen(jnp.maximum(x[f][r].astype(F32), 0.0))

    def first(f, r, n):
        h = jnp.maximum(conv(xw.at[f], r, n, w1), 0.0)
        for k in range(n):
            hw[f, r + k] = widen(h[k * COLS:(k + 1) * COLS])

    def second(f, r, n, acc):
        y = conv(hw.at[f], r, n, w2)
        y = jnp.maximum(y + x[f][r + 2:r + 2 + n].reshape(n * COLS, C).astype(F32), 0.0)
        o[f, r:r + n] = y.reshape(n, COLS, C)
        part = jnp.sum(y.reshape(n * COLS // 8, 8, C), axis=0)
        return part if acc is None else acc + part

    spread(0, range(step1 + 2))
    plan = spans(14, step1)
    done = step1 + 2
    for i, (r, n) in enumerate(plan):
        if i + 1 < len(plan):
            upto = plan[i + 1][0] + plan[i + 1][1] + 2
            spread(0, range(done, upto))
            done = upto
        first(0, r, n)
    cw2.wait(); cx1.wait()
    acc = None
    plan = spans(12, step2)
    for i, (r, n) in enumerate(plan):
        spread(1, range(i * 16 // len(plan), (i + 1) * 16 // len(plan)))
        acc = second(0, r, n, acc)
    sum_ref[0] = acc
    cout = pltpu.make_async_copy(o.at[0], out_hbm.at[0, 0, pl.ds(2, ROWS - 4)], sems.at[4])
    cout.start()
    for r, n in spans(14, step1):
        first(1, r, n)
    acc = None
    for r, n in spans(12, step2):
        acc = second(1, r, n, acc)
    sum_ref[1] = acc
    csp.wait(); cgp.wait(); cout.wait()


def interior(x0, w1, g, w2, sp, gp, step1=7, step2=4):
    proj = jax.ShapeDtypeStruct((C, E), BF)
    return pl.pallas_call(
        functools.partial(interior_kernel, step1, step2),
        name="interior_rows",
        out_shape=(jax.ShapeDtypeStruct((2, ROWS, COLS, 3 * C), BF),
                   jax.ShapeDtypeStruct((2, 14, COLS, 3 * C), BF),
                   jax.ShapeDtypeStruct((2, 12, COLS, C), F32),
                   jax.ShapeDtypeStruct((2, 8, C), F32), jax.ShapeDtypeStruct(x0.shape, BF),
                   jax.ShapeDtypeStruct(w2.shape, BF), proj, proj,
                   jax.ShapeDtypeStruct((2, 1, ROWS, COLS, C), F32)),
        in_specs=[VM] * 2 + [HBM] * 4,
        out_specs=(VM,) * 8 + (HBM,),
        scratch_shapes=[pltpu.SemaphoreType.DMA((5,))],
        compiler_params=pltpu.CompilerParams(vmem_limit_bytes=24 * MIB),
        cost_estimate=pl.CostEstimate(flops=4_200_000_000, transcendentals=0, bytes_accessed=6_000_000),
    )(x0, w1, *in_hbm(g, w2, sp, gp))


def edge_kernel(label, sharp, cross, chip, x0, x1, xw, hw, sums, w1, w2, inner, partial_hbm,
                o, copies, temp, out_hbm, halo, hh, sem):
    cout = pltpu.make_async_copy(inner.at[1], out_hbm.at[1, 0, pl.ds(2, ROWS - 4)], sem)
    cout.start()
    temp[...] = jnp.full((8, 128), sharp[0], F32)
    here, strips = lax.axis_index("strip"), lax.axis_size("strip")
    odd = lax.rem(here, 2)
    for f in range(2):
        for r in range(2):
            halo[2 * f + 1 - odd, r] = widen(jnp.maximum(chip[f, r].astype(F32), 0.0))
            halo[2 * f + odd, r] = widen(jnp.maximum(cross[f, r].astype(F32), 0.0))
    for k in range(4):
        f = k // 2
        if k % 2 == 0:
            rows = [halo[k, 0], halo[k, 1], xw[f, 0], xw[f, 1]]
        else:
            rows = [xw[f, ROWS - 2], xw[f, ROWS - 1], halo[k, 0], halo[k, 1]]
        h = jnp.maximum(conv_of(rows, w1), 0.0)
        for r in range(2):
            row = h[r * COLS:(r + 1) * COLS]
            if k % 2 == 0 and r == 0:
                row = jnp.where(here > 0, row, 0.0)
            if k % 2 == 1 and r == 1:
                row = jnp.where(here < strips - 1, row, 0.0)
            hh[k, r] = widen(row)
    tot = [sums[0], sums[1]]
    for k in range(4):
        f = k // 2
        if k % 2 == 0:
            rows = [hh[k, 0], hh[k, 1], hw[f, 0], hw[f, 1]]
        else:
            rows = [hw[f, 12], hw[f, 13], hh[k, 0], hh[k, 1]]
        y = conv_of(rows, w2)
        y = jnp.maximum(y + (x0, x1)[f][0, 14 * (k % 2):14 * (k % 2) + 2].reshape(2 * COLS, C).astype(F32), 0.0)
        o[k] = y.reshape(2, COLS, C)
        tot[f] = tot[f] + jnp.sum(y.reshape(16, 8, C), axis=0)
    scale = 1.0 / (strips * ROWS * COLS)
    mark = jnp.full((1, 128), label[0], jnp.int32).astype(F32) * (1.0 / strips)
    both = jnp.concatenate(
        [jnp.concatenate([jnp.sum(tot[f], axis=0, keepdims=True) * scale, mark], axis=1) for f in range(2)], axis=0).astype(BF)
    for n in range(copies.shape[0]):
        copies[n] = both
    cout.wait()


def edges(label, sharp, cross, chip, x0, x1, xw, hw, sums, w1, w2, inner, out, members):
    return pl.pallas_call(
        edge_kernel,
        name="edge_rows",
        out_shape=(jax.ShapeDtypeStruct((4, 2, COLS, C), F32), jax.ShapeDtypeStruct((members, 2, C + 128), BF),
                   jax.ShapeDtypeStruct((8, 128), F32), jax.ShapeDtypeStruct(out.shape, F32)),
        in_specs=[SM] * 2 + [VM] * 10 + [HBM],
        out_specs=(VM, VM, VM, HBM),
        input_output_aliases={12: 3},
        scratch_shapes=[
            pltpu.VMEM((4, 2, COLS, 3 * C), BF),
            pltpu.VMEM((4, 2, COLS, 3 * C), BF),
            pltpu.SemaphoreType.DMA,
        ],
        compiler_params=pltpu.CompilerParams(vmem_limit_bytes=24 * MIB),
        cost_estimate=pl.CostEstimate(flops=1_200_000_000, transcendentals=0, bytes_accessed=4_000_000),
    )(label, sharp, cross, chip, x0, x1, xw, hw, sums, w1, w2, inner, out)


def head_kernel(sharp, tot, sproj, gproj, oe, partial_hbm, loss_ref, gs_hbm, gg_hbm, out_hbm, buf, sem, osem):
    outs = []
    for k in range(4):
        outs.append(pltpu.make_async_copy(oe.at[k], out_hbm.at[k // 2, 0, pl.ds((ROWS - 2) * (k % 2), 2)], osem.at[k]))
        outs[-1].start()
    pairs = tot.shape[1]
    s_pool = tot[0, :, :C].astype(BF)
    g_pool = tot[1, :, :C].astype(BF)
    label = tot[0, :, C:C + 1]
    temp = sharp[0:1, 0:1]
    s_emb = jnp.dot(s_pool, sproj[...], preferred_element_type=F32)
    g_emb = jnp.dot(g_pool, gproj[...], preferred_element_type=F32)
    s_inv = lax.rsqrt(jnp.sum(s_emb * s_emb, axis=-1, keepdims=True) + 1e-06)
    g_inv = lax.rsqrt(jnp.sum(g_emb * g_emb, axis=-1, keepdims=True) + 1e-06)
    s_unit = s_emb * s_inv
    g_unit = g_emb * g_inv
    s_bf = s_unit.astype(BF)
    g_bf = g_unit.astype(BF)
    logits = temp * lax.dot_general(s_bf, g_bf, (((1,), (1,)), ((), ())), preferred_element_type=F32)
    ex = jnp.exp(logits)
    row_total = jnp.sum(ex, axis=1, keepdims=True)
    column = lax.broadcasted_iota(jnp.int32, (pairs, pairs), 1).astype(F32)
    matched = column == label
    lgrad = (ex / row_total - jnp.where(matched, 1.0, 0.0)).astype(BF)

    def finish(k, unit_grad, unit, inverse, pool, dest):
        grad = ((unit_grad - unit * jnp.sum(unit * unit_grad, axis=-1, keepdims=True)) * inverse).astype(BF)
        for p in range(2):
            half = pl.ds(p * (C // 2), C // 2)
            buf[k, half] = lax.dot_general(pool[:, p * (C // 2):(p + 1) * (C // 2)], grad, (((0,), (0,)), ((), ())),
                                           preferred_element_type=F32)
            cp = pltpu.make_async_copy(buf.at[k, half], dest.at[half], sem.at[2 * k + p])
            cp.start()
            outs.append(cp)

    s_ug = temp * jnp.dot(lgrad, g_bf, preferred_element_type=F32)
    finish(0, s_ug, s_unit, s_inv, s_pool, gs_hbm)
    g_ug = temp * lax.dot_general(lgrad, s_bf, (((0,), (0,)), ((), ())), preferred_element_type=F32)
    finish(1, g_ug, g_unit, g_inv, g_pool, gg_hbm)
    positive = jnp.sum(jnp.where(matched, logits, 0.0), axis=1, keepdims=True)
    losses = jnp.log(row_total) - positive
    row = lax.broadcasted_iota(jnp.int32, (pairs, 1), 0)
    loss_ref[0] = jnp.sum(jnp.where(row == lax.axis_index("batch"), losses, 0.0))
    for cp in outs:
        cp.wait()


def head(sharp, tot, sproj, gproj, oe, out):
    return pl.pallas_call(
        head_kernel,
        name="contrastive_head",
        out_shape=(jax.ShapeDtypeStruct((1,), F32), jax.ShapeDtypeStruct((C, E), F32),
                   jax.ShapeDtypeStruct((C, E), F32), jax.ShapeDtypeStruct(out.shape, F32)),
        in_specs=[VM] * 5 + [HBM],
        out_specs=(SM, HBM, HBM, HBM),
        input_output_aliases={5: 3},
        scratch_shapes=[pltpu.VMEM((2, C, E), F32), pltpu.SemaphoreType.DMA((4,)), pltpu.SemaphoreType.DMA((4,))],
        compiler_params=pltpu.CompilerParams(vmem_limit_bytes=16 * MIB),
    )(sharp, tot, sproj, gproj, oe, out)


def gather_groups(batch, strips, inner):
    lines = {}
    for b in range(batch):
        for s in range(strips):
            half, plane = divmod(b, batch // 2)
            lines.setdefault(plane if inner else (half, s), []).append(b * strips + s)
    return list(lines.values())


def shards(state_maps, goal_maps, conv_one, conv_two, state_proj, goal_proj, inv_temp, pair_index):
    strips, batch = lax.axis_size("strip"), lax.axis_size("batch")
    w1 = conv_one.reshape(3, 3 * C, C)
    w2 = conv_two.reshape(3, 3 * C, C)
    cross, chip, x0, w1 = load(state_maps, goal_maps, w1)
    cross = lax.ppermute(cross, "strip", [(i, i + 2 * (i % 2) - 1) for i in range(1, strips - 1)])
    chip = lax.ppermute(chip, "strip", [(i, i ^ 1) for i in range(strips)])
    xw, hw, inner, sums, x1, w2, sp, gp, out = interior(x0, w1, goal_maps, w2, state_proj, goal_proj)
    oe, copies, temp, out = edges(
        pair_index, inv_temp, cross, chip, x0, x1, xw, hw, sums, w1, w2, inner, out, 2 * strips)
    both = ("batch", "strip")
    line = lax.all_to_all(copies, both, 0, 0, tiled=True, axis_index_groups=gather_groups(batch, strips, True))
    means = jnp.sum(line.reshape(2, strips, 2, C + 128).astype(F32), axis=1).astype(BF).reshape(4, C + 128)
    copies = jnp.broadcast_to(means, (batch // 2, 4, C + 128))
    got = lax.all_to_all(copies, both, 0, 0, tiled=True, axis_index_groups=gather_groups(batch, strips, False))
    tot = jnp.transpose(got.reshape(batch // 2, 2, 2, C + 128).astype(F32), (2, 1, 0, 3)).reshape(2, batch, C + 128)
    return head(temp, tot, sp, gp, oe, out)


def solution(mesh):
    placed = (
        P("batch", "strip", None, None),
        P("batch", "strip", None, None),
        P(),
        P(),
        P(),
        P(),
        P(),
        P("batch"),
    )
    return jax.shard_map(
        shards,
        mesh=mesh,
        in_specs=placed,
        out_specs=(P("batch"), P(), P(), P(None, "batch", "strip", None, None)),
        check_vma=False,
    )
```
